32 devices in a mesh: row: 8 (over z, core), col: 4 (over y, x).
Axes of the slice: x: 2, y: 2, z: 4, core: 2. Of those that a mesh axis runs over, the one named last changes fastest.
Arguments:
- matrix: float32 [8192, 4096], P('row', 'col'), may hold values from -6 to 166
Outputs:
- updated: float32 [8192, 4096], P('row', 'col')
The draws below stay inside these ranges and needn't reach their ends.
All inputs are finite; a program needn't handle non-finite values.
Results may differ from the reference program's by a relative error of at most 0.0003.
Values sent between devices are 32-bit elements; how exact they have to be, the bound alone decides.
No kernel may reach another device: no remote copies, remote signals or barrier semaphores. Data moves between devices by JAX's collectives and lax.ppermute only.
A program may use at most 64 MiB of HBM per device.

```python
import math
import jax
import jax.numpy as jnp
from jax import lax

NB = 128
RB = 8
CB = 8
PROWS = 8
PCOLS = 4
ORDER = 8192
WINDOW = 4096


def draw_matrix(key, part):
    base = jnp.clip(jax.random.normal(key, (ORDER, WINDOW), jnp.float32), -6.0, 6.0)
    row_ids = lax.broadcasted_iota(jnp.int32, (ORDER, WINDOW), 0)
    col_ids = lax.broadcasted_iota(jnp.int32, (ORDER, WINDOW), 1)
    boost_value = 0.5 * NB + 3.0 * math.sqrt(NB)
    boost = jnp.where((row_ids == col_ids) & (row_ids < NB), boost_value, 0.0)
    return (base + boost).astype(jnp.float32)


def setup_inputs(seed: int = 0) -> dict:
    keys = jax.random.split(jax.random.key(seed), 2)
    return {
        "matrix": draw_matrix(jax.random.fold_in(keys[1], 71), 0),
    }


def factor(corner):
    symmetric = jnp.tril(corner) + jnp.tril(corner, -1).T
    lower_factor = jnp.linalg.cholesky(symmetric)
    identity = jnp.eye(corner.shape[0], dtype=corner.dtype)
    inverse = jax.scipy.linalg.solve_triangular(lower_factor, identity, lower=True)
    return (lower_factor, inverse)

def reference(matrix):
    rows_total = matrix.shape[0] // NB
    cols_total = matrix.shape[1] // NB
    lower_factor, inverse = factor(matrix[:NB, :NB])
    panel = lax.dot_general(matrix[:, :NB].astype(jnp.float32), inverse.astype(jnp.float32), (((1,), (1,)), ((), ())), precision=lax.Precision.HIGHEST, preferred_element_type=jnp.float32)
    panel = panel.at[:NB].set(lower_factor)
    stored_rows = jnp.arange(rows_total, dtype=jnp.int32)
    global_rows = stored_rows % RB * PROWS + stored_rows // RB
    stored_cols = jnp.arange(cols_total, dtype=jnp.int32)
    global_cols = stored_cols % CB * PCOLS + stored_cols // CB
    source_rows = global_cols % PROWS * RB + global_cols // PROWS
    mirror = panel.reshape(rows_total, NB, NB)[source_rows].reshape(cols_total * NB, NB)

    def one_row(bundle):
        row_block, panel_rows, global_row = bundle
        product = lax.dot_general(panel_rows.astype(jnp.float32), mirror.astype(jnp.float32), (((1,), (1,)), ((), ())), precision=lax.Precision.HIGHEST, preferred_element_type=jnp.float32)
        fresh = row_block - product
        keep_mask = (global_row >= global_cols) & (global_cols >= 1)
        col_mask = jnp.repeat(keep_mask, NB)[None, :]
        result = jnp.where(col_mask, fresh, row_block)
        return result.at[:, :NB].set(panel_rows)
    blocks = matrix.reshape(rows_total, NB, matrix.shape[1])
    output = lax.map(one_row, (blocks, panel.reshape(rows_total, NB, NB), global_rows))
    return output.reshape(matrix.shape)
```

```python
import functools

import jax
import jax.numpy as jnp
from jax import lax
from jax.experimental import pallas as pl
from jax.experimental.pallas import tpu as pltpu
from jax.sharding import PartitionSpec as P

NB = 128
AXES = ("row", "col")
HIGHEST = lax.Precision.HIGHEST
TRANS_B = (((1,), (1,)), ((), ()))


def factor_kernel(place_ref, corner_ref, lower_ref, inverse_ref):
    on_root = (place_ref[0] == 0) & (place_ref[1] == 0)

    @pl.when(jnp.logical_not(on_root))
    def _():
        lower_ref[...] = jnp.zeros_like(lower_ref)
        inverse_ref[...] = jnp.zeros_like(inverse_ref)

    @pl.when(on_root)
    def _():
        rows = lax.broadcasted_iota(jnp.int32, (NB, NB), 0)
        cols = lax.broadcasted_iota(jnp.int32, (NB, NB), 1)
        corner = corner_ref[...]
        left = jnp.where(rows >= cols, corner, corner.T)
        right = jnp.where(rows == cols, 1.0, 0.0).astype(jnp.float32)
        lefts = [left[8 * b:8 * b + 8, :] for b in range(NB // 8)]
        rights = [right[8 * b:8 * b + 8, :] for b in range(NB // 8)]
        sub = lax.broadcasted_iota(jnp.int32, (8, NB), 0)
        for k in range(NB):
            b, o = divmod(k, 8)
            pivot = lefts[b][o:o + 1, k:k + 1]
            inv_pivot = 1.0 / jnp.broadcast_to(pivot, (1, NB))
            row_left = lefts[b][o:o + 1, :]
            row_right = rights[b][o:o + 1, :]
            for i in range(b, NB // 8):
                mult = jnp.broadcast_to(lefts[i][:, k:k + 1], (8, NB)) * inv_pivot
                if i == b:
                    if o == 7:
                        continue
                    mult = jnp.where(sub > o, mult, 0.0)
                lefts[i] = lefts[i] - mult * row_left
                rights[i] = rights[i] - mult * row_right
        upper = jnp.concatenate(lefts, axis=0)
        unit_inverse = jnp.concatenate(rights, axis=0)
        diagonal = jnp.sum(jnp.where(rows == cols, upper, 0.0), axis=1, keepdims=True)
        scale = 1.0 / jnp.sqrt(jnp.broadcast_to(diagonal, (NB, NB)))
        lower_ref[...] = jnp.where(rows >= cols, (upper * scale).T, 0.0)
        inverse_ref[...] = jnp.where(rows >= cols, unit_inverse * scale, 0.0)


def factor(place, corner):
    return pl.pallas_call(
        factor_kernel,
        out_shape=[jax.ShapeDtypeStruct((NB, NB), jnp.float32)] * 2,
        in_specs=[pl.BlockSpec(memory_space=pltpu.SMEM), pl.BlockSpec(memory_space=pltpu.VMEM)],
        out_specs=[pl.BlockSpec(memory_space=pltpu.VMEM)] * 2,
        cost_estimate=pl.CostEstimate(flops=20_000_000, bytes_accessed=200_000, transcendentals=0),
        name="factor",
    )(place, corner)


def split(value):
    high = value.astype(jnp.bfloat16)
    low = (value - high.astype(jnp.float32)).astype(jnp.bfloat16)
    return high, low


def dot_t(a, b):
    return lax.dot_general(a, b, TRANS_B, preferred_element_type=jnp.float32)


def update_kernel(rows_here, cols_here, sources, place_ref, matrix_ref, panel_ref, mirror_ref,
                  inverse_ref, lower_ref, out_ref, high_ref, low_ref):
    step = pl.program_id(0)
    col_blocks = matrix_ref.shape[1] // NB
    each = col_blocks // sources

    @pl.when(step == 0)
    def _():
        mirror = lax.dot_general(mirror_ref[...], inverse_ref[...], TRANS_B, precision=HIGHEST,
                                 preferred_element_type=jnp.float32)
        high, low = split(mirror)
        high_ref[...] = high
        low_ref[...] = low

    panel = lax.dot_general(panel_ref[...], inverse_ref[...], TRANS_B, precision=HIGHEST,
                            preferred_element_type=jnp.float32)
    high, low = split(panel)
    row = step * rows_here + place_ref[0]
    for t in range(col_blocks):
        block = (t % sources) * each + t // sources
        here = pl.ds(block * NB, NB)
        product = dot_t(high, high_ref[here, :]) + (
            dot_t(high, low_ref[here, :]) + dot_t(low, high_ref[here, :]))
        col = t * cols_here + place_ref[1]
        keep = (row >= col) & (col >= 1)
        old = matrix_ref[:, t * NB:(t + 1) * NB]
        new = jnp.where(keep, old - product, old)
        if t == 0:
            factor_block = jnp.where(row == 0, lower_ref[...], panel)
            new = jnp.where(col == 0, factor_block, new)
        out_ref[:, t * NB:(t + 1) * NB] = new


def update(place, matrix, panel, mirror, inverse, lower, rows_here, cols_here, sources):
    height, width = matrix.shape
    whole = lambda shape: pl.BlockSpec(shape, lambda s: (0, 0))
    return pl.pallas_call(
        functools.partial(update_kernel, rows_here, cols_here, sources),
        out_shape=jax.ShapeDtypeStruct(matrix.shape, jnp.float32),
        grid=(height // NB,),
        in_specs=[
            pl.BlockSpec(memory_space=pltpu.SMEM),
            pl.BlockSpec((NB, width), lambda s: (s, 0)),
            pl.BlockSpec((NB, NB), lambda s: (s, 0)),
            whole(mirror.shape),
            whole((NB, NB)),
            whole((NB, NB)),
        ],
        out_specs=pl.BlockSpec((NB, width), lambda s: (s, 0)),
        scratch_shapes=[pltpu.VMEM((width, NB), jnp.bfloat16)] * 2,
        compiler_params=pltpu.CompilerParams(dimension_semantics=("arbitrary",)),
        cost_estimate=pl.CostEstimate(flops=2 * height * width * NB * 3,
                                      bytes_accessed=8 * height * width, transcendentals=0),
        name="update",
    )(place, matrix, panel, mirror, inverse, lower)


def body(matrix):
    rows_here = lax.axis_size("row")
    cols_here = lax.axis_size("col")
    row_index = lax.axis_index("row")
    col_index = lax.axis_index("col")
    col_blocks = matrix.shape[1] // NB
    sources = rows_here // cols_here
    place = jnp.stack([row_index, col_index]).astype(jnp.int32)

    def at(r, c):
        return r * cols_here + c

    column = matrix[:, :NB]
    first = column[:NB * (col_blocks // sources)]

    hop = lax.ppermute(first, AXES, [(at(r, 0), at(r ^ 1, r % cols_here)) for r in range(rows_here)])

    panels = []
    held = {0: column}
    step = 1
    while step < cols_here:
        merged = sum(held.values()) if len(held) > 1 else column
        base = range(0, step)
        near = lax.ppermute(merged, "col", [(h, h + step) for h in base])
        panels.append(near)
        if 2 * step < cols_here:
            far = lax.ppermute(merged, "col", [(h, h + 2 * step) for h in base])
            panels.append(far)
            relays = near + far
            pairs = [(at(r, h + (step if r % 2 == 0 else 2 * step)), at(r, h + 3 * step))
                     for r in range(rows_here) for h in base]
            panels.append(lax.ppermute(relays, AXES, pairs))
        held = {0: jnp.where(col_index == 0, column, 0.0), **dict(enumerate(panels, 1))}
        step *= 4

    lower, inverse = factor(place, matrix[:NB, :NB])

    own = [((r ^ 1) % cols_here, r) for r in range(rows_here)]
    mirrors = [[] for _ in range(sources)]
    for k in range(1, rows_here):
        got = lax.ppermute(hop, AXES, [(at(r, c), at((r + k) % rows_here, c)) for c, r in own])
        for q in range(sources):
            origin = (row_index - k) % rows_here
            mine = (origin ^ 1) == col_index + q * cols_here
            mirrors[q].append(jnp.where(mine, got, 0.0))
    for q in range(sources):
        mirrors[q].append(jnp.where((row_index ^ 1) == col_index + q * cols_here, hop, 0.0))
    mirror = jnp.concatenate([sum(parts) for parts in mirrors], axis=0)

    holders = [(0, 0)]
    offsets = []
    bit = rows_here // 2
    while bit >= 2:
        offsets.append((bit, 0))
        bit //= 2
    bit = cols_here // 2
    while bit >= 1:
        offsets.append((0, bit))
        bit //= 2
    offsets.append((1, 0))
    for dr, dc in offsets:
        inverse = inverse + lax.ppermute(
            inverse, AXES, [(at(r, c), at(r + dr, c + dc)) for r, c in holders])
        holders = holders + [(r + dr, c + dc) for r, c in holders]

    panel = jnp.where(col_index == 0, column, 0.0) + sum(panels)
    return update(place, matrix, panel, mirror, inverse, lower, rows_here, cols_here, sources)


def solution(mesh):
    return jax.shard_map(
        body,
        mesh=mesh,
        in_specs=(P("row", "col"),),
        out_specs=P("row", "col"),
        check_vma=False,
    )
```

```python
import functools

import jax
import jax.numpy as jnp
from jax import lax
from jax.experimental import pallas as pl
from jax.experimental.pallas import tpu as pltpu
from jax.sharding import PartitionSpec as P

NB = 128
TILE = 256
AXES = ("row", "col")
HIGHEST = lax.Precision.HIGHEST
TRANS_B = (((1,), (1,)), ((), ()))


def factor_kernel(corner_ref, lower_ref, inverse_ref):
    rows = lax.broadcasted_iota(jnp.int32, (NB, NB), 0)
    cols = lax.broadcasted_iota(jnp.int32, (NB, NB), 1)
    corner = corner_ref[...]
    left = jnp.where(rows >= cols, corner, corner.T)
    right = jnp.where(rows == cols, 1.0, 0.0).astype(jnp.float32)
    lefts = [left[8 * b:8 * b + 8, :] for b in range(NB // 8)]
    rights = [right[8 * b:8 * b + 8, :] for b in range(NB // 8)]
    sub = lax.broadcasted_iota(jnp.int32, (8, NB), 0)
    for k in range(NB):
        b, o = divmod(k, 8)
        pivot = lefts[b][o:o + 1, k:k + 1]
        inv_pivot = 1.0 / jnp.broadcast_to(pivot, (1, NB))
        row_left = lefts[b][o:o + 1, :]
        row_right = rights[b][o:o + 1, :]
        for i in range(b, NB // 8):
            mult = jnp.broadcast_to(lefts[i][:, k:k + 1], (8, NB)) * inv_pivot
            if i == b:
                if o == 7:
                    continue
                mult = jnp.where(sub > o, mult, 0.0)
            lefts[i] = lefts[i] - mult * row_left
            rights[i] = rights[i] - mult * row_right
    upper = jnp.concatenate(lefts, axis=0)
    unit_inverse = jnp.concatenate(rights, axis=0)
    diagonal = jnp.sum(jnp.where(rows == cols, upper, 0.0), axis=1, keepdims=True)
    scale = 1.0 / jnp.sqrt(jnp.broadcast_to(diagonal, (NB, NB)))
    lower_ref[...] = jnp.where(rows >= cols, (upper * scale).T, 0.0)
    inverse_ref[...] = jnp.where(rows >= cols, unit_inverse * scale, 0.0)


def factor(corner):
    return pl.pallas_call(
        factor_kernel,
        out_shape=[jax.ShapeDtypeStruct((NB, NB), jnp.float32)] * 2,
        in_specs=[pl.BlockSpec(memory_space=pltpu.VMEM)],
        out_specs=[pl.BlockSpec(memory_space=pltpu.VMEM)] * 2,
        compiler_params=pltpu.CompilerParams(vmem_limit_bytes=4 * 1024 * 1024),
        cost_estimate=pl.CostEstimate(flops=4_000_000_000, bytes_accessed=40_000_000, transcendentals=0),
        name="factor",
    )(corner)


def split(value):
    high = value.astype(jnp.bfloat16)
    low = (value - high.astype(jnp.float32)).astype(jnp.bfloat16)
    return high, low


def update_kernel(plan, *refs):
    rows_here, cols_here, sources, arrivals, hops = plan
    n_panel, n_mirror = len(arrivals) + 1, hops
    lower_ref, inverse_ref, matrix_ref = refs[:3]
    panel_refs = refs[3:3 + n_panel - 1]
    mirror_refs = refs[3 + n_panel - 1:3 + n_panel - 1 + n_mirror]
    out_ref, old, new, panel, mirror, rhs, in_sems, panel_sems, mirror_sems, out_sems = refs[3 + n_panel - 1 + n_mirror:]
    row_index = lax.axis_index("row")
    col_index = lax.axis_index("col")
    height, width = old.shape
    col_blocks = width // NB
    each = mirror.shape[0] // sources
    tiles = height // TILE
    here = [pl.ds(i * TILE, TILE) for i in range(tiles)]

    pairs = rows_here // 2
    for q in range(sources):
        away = lax.rem(row_index // 2 - (col_index + q * cols_here) // 2 + pairs, pairs)
        for d in range(hops):
            @pl.when(away == d)
            def _(d=d, q=q):
                pltpu.make_async_copy(mirror_refs[d], mirror.at[pl.ds(q * each, each)], mirror_sems.at[q]).start()

    def fetch_panel(source, i):
        pltpu.make_async_copy(source, panel.at[here[i]], panel_sems.at[i]).start()

    for i in range(tiles):
        @pl.when(col_index == 0)
        def _(i=i):
            fetch_panel(matrix_ref.at[here[i], pl.ds(0, NB)], i)
        for n, columns in enumerate(arrivals):
            mine = functools.reduce(jnp.logical_or, [col_index == c for c in columns])

            @pl.when(mine)
            def _(i=i, n=n):
                fetch_panel(panel_refs[n].at[here[i]], i)
        pltpu.make_async_copy(matrix_ref.at[here[i]], old.at[here[i]], in_sems.at[i]).start()

    for q in range(sources):
        pltpu.make_async_copy(mirror_refs[0], mirror.at[pl.ds(q * each, each)], mirror_sems.at[q]).wait()
    for t in range(col_blocks):
        block = (t % sources) * each + (t // sources) * NB
        part = lax.dot_general(inverse_ref[...], mirror[pl.ds(block, NB), :], TRANS_B, precision=HIGHEST,
                               preferred_element_type=jnp.float32)
        high, low = split(part)
        at = pl.ds(t * NB, NB)
        rhs[pl.ds(0, NB), at] = high
        rhs[pl.ds(NB, NB), at] = high
        rhs[pl.ds(2 * NB, NB), at] = low

    for i in range(tiles):
        pltpu.make_async_copy(matrix_ref.at[here[i], pl.ds(0, NB)], panel.at[here[i]], panel_sems.at[i]).wait()
        tall = lax.dot_general(panel[here[i], :], inverse_ref[...], TRANS_B, precision=HIGHEST,
                               preferred_element_type=jnp.float32)
        high, low = split(tall)
        lhs = jnp.concatenate([high, low, high], axis=1)
        product = jnp.dot(lhs, rhs[...], preferred_element_type=jnp.float32)
        pltpu.make_async_copy(matrix_ref.at[here[i]], old.at[here[i]], in_sems.at[i]).wait()
        for s in range(TILE // NB):
            row = (i * (TILE // NB) + s) * rows_here + row_index
            down = pl.ds(i * TILE + s * NB, NB)
            for t in range(col_blocks):
                across = pl.ds(t * NB, NB)
                col = t * cols_here + col_index
                before = old[down, across]
                after = before - product[s * NB:(s + 1) * NB, t * NB:(t + 1) * NB]
                value = jnp.where((row >= col) & (col >= 1), after, before)
                if t == 0:
                    block = jnp.where(row == 0, lower_ref[...], tall[s * NB:(s + 1) * NB, :])
                    value = jnp.where(col == 0, block, value)
                new[down, across] = value
        pltpu.make_async_copy(new.at[here[i]], out_ref.at[here[i]], out_sems.at[i]).start()
    for i in range(tiles):
        pltpu.make_async_copy(new.at[here[i]], out_ref.at[here[i]], out_sems.at[i]).wait()


def update(lower, inverse, matrix, panels, mirrors, plan):
    height, width = matrix.shape
    sources = plan[2]
    tiles = height // TILE
    vmem = pl.BlockSpec(memory_space=pltpu.VMEM)
    anywhere = pl.BlockSpec(memory_space=pl.ANY)
    return pl.pallas_call(
        functools.partial(update_kernel, plan),
        out_shape=jax.ShapeDtypeStruct(matrix.shape, jnp.float32),
        in_specs=[vmem, vmem, pl.BlockSpec(memory_space=pltpu.HBM)] + [anywhere] * (len(panels) + len(mirrors)),
        out_specs=anywhere,
        scratch_shapes=[
            pltpu.VMEM((height, width), jnp.float32),
            pltpu.VMEM((height, width), jnp.float32),
            pltpu.VMEM((height, NB), jnp.float32),
            pltpu.VMEM((width, NB), jnp.float32),
            pltpu.VMEM((3 * NB, width), jnp.bfloat16),
            pltpu.SemaphoreType.DMA((tiles,)),
            pltpu.SemaphoreType.DMA((tiles,)),
            pltpu.SemaphoreType.DMA((sources,)),
            pltpu.SemaphoreType.DMA((tiles,)),
        ],
        compiler_params=pltpu.CompilerParams(vmem_limit_bytes=16 * 1024 * 1024),
        cost_estimate=pl.CostEstimate(flops=2 * height * width * NB * 3,
                                      bytes_accessed=8 * height * width, transcendentals=0),
        name="update",
    )(lower, inverse, matrix, *panels, *mirrors)


def body(matrix):
    rows_here = lax.axis_size("row")
    cols_here = lax.axis_size("col")
    row_index = lax.axis_index("row")
    col_index = lax.axis_index("col")
    col_blocks = matrix.shape[1] // NB
    sources = rows_here // cols_here
    every_row = range(rows_here)

    def at(r, c):
        return r * cols_here + c

    corner = jnp.where((row_index == 0) & (col_index == 0), matrix[:NB, :NB], 0.0)
    holders = [(0, 0)]
    offsets = [(0, 1 << b) for b in range(cols_here.bit_length() - 1)]
    offsets += [(1 << b, 0) for b in reversed(range(rows_here.bit_length() - 1))]
    for dr, dc in offsets:
        corner = corner + lax.ppermute(corner, AXES, [(at(r, c), at(r + dr, c + dc)) for r, c in holders])
        holders = holders + [(r + dr, c + dc) for r, c in holders]

    column = matrix[:, :NB]
    first = column[:NB * (col_blocks // sources)]

    hop = lax.ppermute(first, AXES, [(at(r, 0), at(r ^ 1, r % cols_here)) for r in every_row])
    hop += lax.ppermute(first, AXES, [(at(r, 0), at(r, r % cols_here)) for r in every_row if r % cols_here])
    hop = jnp.where((col_index == 0) & (row_index % cols_here == 0), first, hop)
    mirrors = [hop]
    pairs = rows_here // 2
    for d in range(1, pairs):
        mirrors.append(lax.ppermute(hop, AXES, [
            (at(r, c), at((r + 2 * d) % rows_here, c))
            for r in every_row for c in range(cols_here) if r // 2 in [(c + q * cols_here) // 2 for q in range(sources)]]))

    panels, arrivals = [], []
    merged = column
    step = 1
    while step < cols_here:
        base = range(step)
        near = lax.ppermute(merged, "col", [(h, h + step) for h in base])
        panels.append(near)
        arrivals.append([h + step for h in base])
        if 2 * step < cols_here:
            far = lax.ppermute(merged, "col", [(h, h + 2 * step) for h in base])
            relay = [(at(r, h + (step if r % 2 == 0 else 2 * step)), at(r, h + 3 * step))
                     for r in every_row for h in base]
            last = lax.ppermute(near + far, AXES, relay)
            panels += [far, last]
            arrivals += [[h + 2 * step for h in base], [h + 3 * step for h in base]]
        step *= 4
        if step < cols_here:
            merged = jnp.where(col_index == 0, column, 0.0) + sum(panels)

    lower, inverse = factor(corner)
    return update(lower, inverse, matrix, panels, mirrors, (rows_here, cols_here, sources, arrivals, pairs))


def solution(mesh):
    return jax.shard_map(
        body,
        mesh=mesh,
        in_specs=(P("row", "col"),),
        out_specs=P("row", "col"),
        check_vma=False,
    )
```

```python
import functools

import jax
import jax.numpy as jnp
from jax import lax
from jax.experimental import pallas as pl
from jax.experimental.pallas import tpu as pltpu
from jax.sharding import PartitionSpec as P

NB = 128
TILE = 256
AXES = ("row", "col")
HIGHEST = lax.Precision.HIGHEST
TRANS_B = (((1,), (1,)), ((), ()))


def factor_kernel(corner_ref, lower_ref, inverse_ref):
    rows = lax.broadcasted_iota(jnp.int32, (NB, NB), 0)
    cols = lax.broadcasted_iota(jnp.int32, (NB, NB), 1)
    corner = corner_ref[...]
    left = jnp.where(rows >= cols, corner, corner.T)
    right = jnp.where(rows == cols, 1.0, 0.0).astype(jnp.float32)
    lefts = [left[8 * b:8 * b + 8, :] for b in range(NB // 8)]
    rights = [right[8 * b:8 * b + 8, :] for b in range(NB // 8)]
    sub = lax.broadcasted_iota(jnp.int32, (8, NB), 0)
    for k in range(NB):
        b, o = divmod(k, 8)
        pivot = lefts[b][o:o + 1, k:k + 1]
        inv_pivot = 1.0 / jnp.broadcast_to(pivot, (1, NB))
        row_left = lefts[b][o:o + 1, :]
        row_right = rights[b][o:o + 1, :]
        for i in range(b, NB // 8):
            mult = jnp.broadcast_to(lefts[i][:, k:k + 1], (8, NB)) * inv_pivot
            if i == b:
                if o == 7:
                    continue
                mult = jnp.where(sub > o, mult, 0.0)
            lefts[i] = lefts[i] - mult * row_left
            rights[i] = rights[i] - mult * row_right
    upper = jnp.concatenate(lefts, axis=0)
    unit_inverse = jnp.concatenate(rights, axis=0)
    diagonal = jnp.sum(jnp.where(rows == cols, upper, 0.0), axis=1, keepdims=True)
    scale = 1.0 / jnp.sqrt(jnp.broadcast_to(diagonal, (NB, NB)))
    lower_ref[...] = jnp.where(rows >= cols, (upper * scale).T, 0.0)
    inverse_ref[...] = jnp.where(rows >= cols, unit_inverse * scale, 0.0)


def factor(corner):
    return pl.pallas_call(
        factor_kernel,
        out_shape=[jax.ShapeDtypeStruct((NB, NB), jnp.float32)] * 2,
        in_specs=[pl.BlockSpec(memory_space=pltpu.VMEM)],
        out_specs=[pl.BlockSpec(memory_space=pltpu.VMEM)] * 2,
        compiler_params=pltpu.CompilerParams(vmem_limit_bytes=4 * 1024 * 1024),
        cost_estimate=pl.CostEstimate(flops=4_000_000_000, bytes_accessed=40_000_000, transcendentals=0),
        name="factor",
    )(corner)


def split(value):
    high = value.astype(jnp.bfloat16)
    low = (value - high.astype(jnp.float32)).astype(jnp.bfloat16)
    return high, low


def update_kernel(plan, *refs):
    rows_here, cols_here, sources, arrivals, hops = plan
    n_panel, n_mirror = len(arrivals) + 1, hops
    lower_ref, inverse_ref, matrix_ref = refs[:3]
    panel_refs = refs[3:3 + n_panel - 1]
    mirror_refs = refs[3 + n_panel - 1:3 + n_panel - 1 + n_mirror]
    out_ref, old, new, panel, mirror, rhs, in_sems, panel_sems, mirror_sems, out_sems = refs[3 + n_panel - 1 + n_mirror:]
    row_index = lax.axis_index("row")
    col_index = lax.axis_index("col")
    height, width = old.shape
    col_blocks = width // NB
    each = mirror.shape[0] // sources
    tiles = height // TILE
    here = [pl.ds(i * TILE, TILE) for i in range(tiles)]

    pairs = rows_here // 2
    for q in range(sources):
        away = lax.rem(row_index // 2 - (col_index + q * cols_here) // 2 + pairs, pairs)
        for d in range(hops):
            @pl.when(away == d)
            def _(d=d, q=q):
                pltpu.make_async_copy(mirror_refs[d], mirror.at[pl.ds(q * each, each)], mirror_sems.at[q]).start()

    def fetch_panel(source, i):
        pltpu.make_async_copy(source, panel.at[here[i]], panel_sems.at[i]).start()

    for i in range(tiles):
        @pl.when(col_index == 0)
        def _(i=i):
            fetch_panel(matrix_ref.at[here[i], pl.ds(0, NB)], i)
        for n, columns in enumerate(arrivals):
            mine = functools.reduce(jnp.logical_or, [col_index == c for c in columns])

            @pl.when(mine)
            def _(i=i, n=n):
                fetch_panel(panel_refs[n].at[here[i]], i)
        pltpu.make_async_copy(matrix_ref.at[here[i]], old.at[here[i]], in_sems.at[i]).start()

    for q in range(sources):
        pltpu.make_async_copy(mirror_refs[0], mirror.at[pl.ds(q * each, each)], mirror_sems.at[q]).wait()
    for t in range(col_blocks):
        block = (t % sources) * each + (t // sources) * NB
        part = lax.dot_general(inverse_ref[...], mirror[pl.ds(block, NB), :], TRANS_B, precision=HIGHEST,
                               preferred_element_type=jnp.float32)
        high, low = split(part)
        at = pl.ds(t * NB, NB)
        rhs[pl.ds(0, NB), at] = high
        rhs[pl.ds(NB, NB), at] = high
        rhs[pl.ds(2 * NB, NB), at] = low

    for i in range(tiles):
        pltpu.make_async_copy(matrix_ref.at[here[i], pl.ds(0, NB)], panel.at[here[i]], panel_sems.at[i]).wait()
        tall = lax.dot_general(panel[here[i], :], inverse_ref[...], TRANS_B, precision=HIGHEST,
                               preferred_element_type=jnp.float32)
        high, low = split(tall)
        lhs = jnp.concatenate([high, low, high], axis=1)
        product = jnp.dot(lhs, rhs[...], preferred_element_type=jnp.float32)
        pltpu.make_async_copy(matrix_ref.at[here[i]], old.at[here[i]], in_sems.at[i]).wait()
        for s in range(TILE // NB):
            row = (i * (TILE // NB) + s) * rows_here + row_index
            down = pl.ds(i * TILE + s * NB, NB)
            for t in range(col_blocks):
                across = pl.ds(t * NB, NB)
                col = t * cols_here + col_index
                before = old[down, across]
                after = before - product[s * NB:(s + 1) * NB, t * NB:(t + 1) * NB]
                value = jnp.where((row >= col) & (col >= 1), after, before)
                if t == 0:
                    block = jnp.where(row == 0, lower_ref[...], tall[s * NB:(s + 1) * NB, :])
                    value = jnp.where(col == 0, block, value)
                new[down, across] = value
        pltpu.make_async_copy(new.at[here[i]], out_ref.at[here[i]], out_sems.at[i]).start()
    for i in range(tiles):
        pltpu.make_async_copy(new.at[here[i]], out_ref.at[here[i]], out_sems.at[i]).wait()


def update(lower, inverse, matrix, panels, mirrors, plan):
    height, width = matrix.shape
    sources = plan[2]
    tiles = height // TILE
    vmem = pl.BlockSpec(memory_space=pltpu.VMEM)
    anywhere = pl.BlockSpec(memory_space=pl.ANY)
    return pl.pallas_call(
        functools.partial(update_kernel, plan),
        out_shape=jax.ShapeDtypeStruct(matrix.shape, jnp.float32),
        in_specs=[vmem, vmem, pl.BlockSpec(memory_space=pltpu.HBM)] + [anywhere] * (len(panels) + len(mirrors)),
        out_specs=anywhere,
        scratch_shapes=[
            pltpu.VMEM((height, width), jnp.float32),
            pltpu.VMEM((height, width), jnp.float32),
            pltpu.VMEM((height, NB), jnp.float32),
            pltpu.VMEM((width, NB), jnp.float32),
            pltpu.VMEM((3 * NB, width), jnp.bfloat16),
            pltpu.SemaphoreType.DMA((tiles,)),
            pltpu.SemaphoreType.DMA((tiles,)),
            pltpu.SemaphoreType.DMA((sources,)),
            pltpu.SemaphoreType.DMA((tiles,)),
        ],
        compiler_params=pltpu.CompilerParams(vmem_limit_bytes=16 * 1024 * 1024),
        cost_estimate=pl.CostEstimate(flops=2 * height * width * NB * 3,
                                      bytes_accessed=8 * height * width, transcendentals=0),
        name="update",
    )(lower, inverse, matrix, *panels, *mirrors)


def body(matrix):
    rows_here = lax.axis_size("row")
    cols_here = lax.axis_size("col")
    row_index = lax.axis_index("row")
    col_index = lax.axis_index("col")
    col_blocks = matrix.shape[1] // NB
    sources = rows_here // cols_here
    every_row = range(rows_here)

    def at(r, c):
        return r * cols_here + c

    corner = jnp.where((row_index == 0) & (col_index == 0), matrix[:NB, :NB], 0.0)
    column = matrix[:, :NB]
    first = column[:NB * (col_blocks // sources)]
    holders = [(0, 0)]
    offsets = [(0, 1 << b) for b in range(cols_here.bit_length() - 1)]
    offsets += [(1 << b, 0) for b in reversed(range(rows_here.bit_length() - 1))]
    for dr, dc in offsets:
        corner = corner + lax.ppermute(corner, AXES, [(at(r, c), at(r + dr, c + dc)) for r, c in holders])
        holders = holders + [(r + dr, c + dc) for r, c in holders]
        if len(holders) == cols_here:
            corner, column, first = lax.optimization_barrier((corner, column, first))

    hop = lax.ppermute(first, AXES, [(at(r, 0), at(r ^ 1, r % cols_here)) for r in every_row])
    hop += lax.ppermute(first, AXES, [(at(r, 0), at(r, r % cols_here)) for r in every_row if r % cols_here])
    hop = jnp.where((col_index == 0) & (row_index % cols_here == 0), first, hop)
    mirrors = [hop]
    pairs = rows_here // 2
    for d in range(1, pairs):
        mirrors.append(lax.ppermute(hop, AXES, [
            (at(r, c), at((r + 2 * d) % rows_here, c))
            for r in every_row for c in range(cols_here) if r // 2 in [(c + q * cols_here) // 2 for q in range(sources)]]))

    panels, arrivals = [], []
    merged = column
    step = 1
    while step < cols_here:
        base = range(step)
        near = lax.ppermute(merged, "col", [(h, h + step) for h in base])
        panels.append(near)
        arrivals.append([h + step for h in base])
        if 2 * step < cols_here:
            far = lax.ppermute(merged, "col", [(h, h + 2 * step) for h in base])
            relay = [(at(r, h + (step if r % 2 == 0 else 2 * step)), at(r, h + 3 * step))
                     for r in every_row for h in base]
            last = lax.ppermute(near + far, AXES, relay)
            panels += [far, last]
            arrivals += [[h + 2 * step for h in base], [h + 3 * step for h in base]]
        step *= 4
        if step < cols_here:
            merged = jnp.where(col_index == 0, column, 0.0) + sum(panels)

    lower, inverse = factor(corner)
    return update(lower, inverse, matrix, panels, mirrors, (rows_here, cols_here, sources, arrivals, pairs))


def solution(mesh):
    return jax.shard_map(
        body,
        mesh=mesh,
        in_specs=(P("row", "col"),),
        out_specs=P("row", "col"),
        check_vma=False,
    )
```

```python
import functools

import jax
import jax.numpy as jnp
from jax import lax
from jax.experimental import pallas as pl
from jax.experimental.pallas import tpu as pltpu
from jax.sharding import PartitionSpec as P

NB = 128
TILE = 256
AXES = ("row", "col")
HIGHEST = lax.Precision.HIGHEST
TRANS_B = (((1,), (1,)), ((), ()))


def factor_kernel(corner_ref, lower_ref, inverse_ref):
    rows = lax.broadcasted_iota(jnp.int32, (NB, NB), 0)
    cols = lax.broadcasted_iota(jnp.int32, (NB, NB), 1)
    corner = corner_ref[...]
    left = jnp.where(rows >= cols, corner, corner.T)
    right = jnp.where(rows == cols, 1.0, 0.0).astype(jnp.float32)
    lefts = [left[8 * b:8 * b + 8, :] for b in range(NB // 8)]
    rights = [right[8 * b:8 * b + 8, :] for b in range(NB // 8)]
    sub = lax.broadcasted_iota(jnp.int32, (8, NB), 0)
    for k in range(NB):
        b, o = divmod(k, 8)
        pivot = lefts[b][o:o + 1, k:k + 1]
        inv_pivot = 1.0 / jnp.broadcast_to(pivot, (1, NB))
        row_left = lefts[b][o:o + 1, :]
        row_right = rights[b][o:o + 1, :]
        for i in range(b, NB // 8):
            mult = jnp.broadcast_to(lefts[i][:, k:k + 1], (8, NB)) * inv_pivot
            if i == b:
                if o == 7:
                    continue
                mult = jnp.where(sub > o, mult, 0.0)
            lefts[i] = lefts[i] - mult * row_left
            rights[i] = rights[i] - mult * row_right
    upper = jnp.concatenate(lefts, axis=0)
    unit_inverse = jnp.concatenate(rights, axis=0)
    diagonal = jnp.sum(jnp.where(rows == cols, upper, 0.0), axis=1, keepdims=True)
    scale = 1.0 / jnp.sqrt(jnp.broadcast_to(diagonal, (NB, NB)))
    lower_ref[...] = jnp.where(rows >= cols, (upper * scale).T, 0.0)
    inverse_ref[...] = jnp.where(rows >= cols, unit_inverse * scale, 0.0)


def factor(corner):
    return pl.pallas_call(
        factor_kernel,
        out_shape=[jax.ShapeDtypeStruct((NB, NB), jnp.float32)] * 2,
        in_specs=[pl.BlockSpec(memory_space=pltpu.VMEM)],
        out_specs=[pl.BlockSpec(memory_space=pltpu.VMEM)] * 2,
        compiler_params=pltpu.CompilerParams(vmem_limit_bytes=4 * 1024 * 1024),
        cost_estimate=pl.CostEstimate(flops=4_000_000_000, bytes_accessed=40_000_000, transcendentals=0),
        name="factor",
    )(corner)


def split(value):
    high = value.astype(jnp.bfloat16)
    low = (value - high.astype(jnp.float32)).astype(jnp.bfloat16)
    return high, low


def update_kernel(plan, *refs):
    rows_here, cols_here, sources, arrivals = plan
    n_panel = len(arrivals)
    lower_ref, inverse_ref, matrix_ref = refs[:3]
    panel_refs = refs[3:3 + n_panel]
    mirror_refs = refs[3 + n_panel:3 + n_panel + sources]
    out_ref, old, new, panel, mirror, rhs, in_sems, panel_sems, mirror_sems, out_sems = refs[3 + n_panel + sources:]
    row_index = lax.axis_index("row")
    col_index = lax.axis_index("col")
    height, width = old.shape
    col_blocks = width // NB
    each = mirror.shape[0] // sources
    tiles = height // TILE
    here = [pl.ds(i * TILE, TILE) for i in range(tiles)]

    for q in range(sources):
        away = lax.rem(q - row_index // cols_here + sources, sources)
        for d in range(sources):
            @pl.when(away == d)
            def _(d=d, q=q):
                pltpu.make_async_copy(mirror_refs[d], mirror.at[pl.ds(q * each, each)], mirror_sems.at[q]).start()

    def fetch_panel(source, i):
        pltpu.make_async_copy(source, panel.at[here[i]], panel_sems.at[i]).start()

    for i in range(tiles):
        @pl.when(col_index == 0)
        def _(i=i):
            fetch_panel(matrix_ref.at[here[i], pl.ds(0, NB)], i)
        for n, columns in enumerate(arrivals):
            mine = functools.reduce(jnp.logical_or, [col_index == c for c in columns])

            @pl.when(mine)
            def _(i=i, n=n):
                fetch_panel(panel_refs[n].at[here[i]], i)
        pltpu.make_async_copy(matrix_ref.at[here[i]], old.at[here[i]], in_sems.at[i]).start()

    for q in range(sources):
        pltpu.make_async_copy(mirror_refs[0], mirror.at[pl.ds(q * each, each)], mirror_sems.at[q]).wait()
    for t in range(col_blocks):
        block = (t % sources) * each + (t // sources) * NB
        part = lax.dot_general(inverse_ref[...], mirror[pl.ds(block, NB), :], TRANS_B, precision=HIGHEST,
                               preferred_element_type=jnp.float32)
        high, low = split(part)
        at = pl.ds(t * NB, NB)
        rhs[pl.ds(0, NB), at] = high
        rhs[pl.ds(NB, NB), at] = high
        rhs[pl.ds(2 * NB, NB), at] = low

    for i in range(tiles):
        pltpu.make_async_copy(matrix_ref.at[here[i], pl.ds(0, NB)], panel.at[here[i]], panel_sems.at[i]).wait()
        tall = lax.dot_general(panel[here[i], :], inverse_ref[...], TRANS_B, precision=HIGHEST,
                               preferred_element_type=jnp.float32)
        high, low = split(tall)
        lhs = jnp.concatenate([high, low, high], axis=1)
        product = jnp.dot(lhs, rhs[...], preferred_element_type=jnp.float32)
        pltpu.make_async_copy(matrix_ref.at[here[i]], old.at[here[i]], in_sems.at[i]).wait()
        for s in range(TILE // NB):
            row = (i * (TILE // NB) + s) * rows_here + row_index
            down = pl.ds(i * TILE + s * NB, NB)
            for t in range(col_blocks):
                across = pl.ds(t * NB, NB)
                col = t * cols_here + col_index
                before = old[down, across]
                after = before - product[s * NB:(s + 1) * NB, t * NB:(t + 1) * NB]
                value = jnp.where((row >= col) & (col >= 1), after, before)
                if t == 0:
                    block = jnp.where(row == 0, lower_ref[...], tall[s * NB:(s + 1) * NB, :])
                    value = jnp.where(col == 0, block, value)
                new[down, across] = value
        pltpu.make_async_copy(new.at[here[i]], out_ref.at[here[i]], out_sems.at[i]).start()
    for i in range(tiles):
        pltpu.make_async_copy(new.at[here[i]], out_ref.at[here[i]], out_sems.at[i]).wait()


def update(lower, inverse, matrix, panels, mirrors, plan):
    height, width = matrix.shape
    sources = plan[2]
    tiles = height // TILE
    vmem = pl.BlockSpec(memory_space=pltpu.VMEM)
    anywhere = pl.BlockSpec(memory_space=pl.ANY)
    return pl.pallas_call(
        functools.partial(update_kernel, plan),
        out_shape=jax.ShapeDtypeStruct(matrix.shape, jnp.float32),
        in_specs=[vmem, vmem, pl.BlockSpec(memory_space=pltpu.HBM)] + [anywhere] * (len(panels) + len(mirrors)),
        out_specs=anywhere,
        scratch_shapes=[
            pltpu.VMEM((height, width), jnp.float32),
            pltpu.VMEM((height, width), jnp.float32),
            pltpu.VMEM((height, NB), jnp.float32),
            pltpu.VMEM((width, NB), jnp.float32),
            pltpu.VMEM((3 * NB, width), jnp.bfloat16),
            pltpu.SemaphoreType.DMA((tiles,)),
            pltpu.SemaphoreType.DMA((tiles,)),
            pltpu.SemaphoreType.DMA((sources,)),
            pltpu.SemaphoreType.DMA((tiles,)),
        ],
        compiler_params=pltpu.CompilerParams(vmem_limit_bytes=16 * 1024 * 1024),
        cost_estimate=pl.CostEstimate(flops=2 * height * width * NB * 3,
                                      bytes_accessed=8 * height * width, transcendentals=0),
        name="update",
    )(lower, inverse, matrix, *panels, *mirrors)


def body(matrix):
    rows_here = lax.axis_size("row")
    cols_here = lax.axis_size("col")
    row_index = lax.axis_index("row")
    col_index = lax.axis_index("col")
    col_blocks = matrix.shape[1] // NB
    sources = rows_here // cols_here
    every_row = range(rows_here)

    def at(r, c):
        return r * cols_here + c

    column = matrix[:, :NB]
    first = column[:NB * (col_blocks // sources)]
    last = cols_here - 1
    corner = jnp.where((row_index == 0) & (col_index == 0), matrix[:NB, :NB], 0.0)
    corner = corner + lax.ppermute(corner, AXES, [(at(0, 0), at(0, last))])
    corner, column, first = lax.optimization_barrier((corner, column, first))
    holders = [(0, last)]
    hops = [(1 << b, 0) for b in reversed(range(rows_here.bit_length() - 1))]
    hops += [(0, 1 << b) for b in range(cols_here.bit_length() - 1)]
    for dr, dc in hops:
        pairs = [(at(r, c), at(r + dr, c - dc)) for r, c in holders if (r + dr, c - dc) != (0, 0)]
        corner = corner + lax.ppermute(corner, AXES, pairs)
        holders = holders + [(r + dr, c - dc) for r, c in holders]

    hop = lax.ppermute(first, AXES, [(at(r, 0), at(r ^ 1, r % cols_here)) for r in every_row])
    hop += lax.ppermute(first, AXES, [(at(r, 0), at(r, r % cols_here)) for r in every_row if r % cols_here])
    hop = jnp.where((col_index == 0) & (row_index % cols_here == 0), first, hop)
    own = [(c + q * cols_here, c) for c in range(cols_here) for q in range(sources)]
    own = own + [(r ^ 1, c) for r, c in own]
    for bit in (1 << b for b in range(1, cols_here.bit_length() - 1)):
        hop = hop + lax.ppermute(hop, AXES, [(at(r, c), at(r ^ bit, c)) for r, c in own])
        own = own + [(r ^ bit, c) for r, c in own]
    mirrors = [hop]
    for q in range(1, sources):
        mirrors.append(lax.ppermute(hop, "row", [((r + q * cols_here) % rows_here, r) for r in every_row]))

    panels, arrivals = [], []
    merged = column
    step = 1
    while step < cols_here:
        base = range(step)
        near = lax.ppermute(merged, "col", [(h, h + step) for h in base])
        panels.append(near)
        arrivals.append([h + step for h in base])
        if 2 * step < cols_here:
            far = lax.ppermute(merged, "col", [(h, h + 2 * step) for h in base])
            relay = [(at(r, h + (step if r % 2 == 0 else 2 * step)), at(r, h + 3 * step))
                     for r in every_row for h in base]
            panels += [far, lax.ppermute(near + far, AXES, relay)]
            arrivals += [[h + 2 * step for h in base], [h + 3 * step for h in base]]
        step *= 4
        if step < cols_here:
            merged = jnp.where(col_index == 0, column, 0.0) + sum(panels)

    lower, inverse = factor(corner)
    return update(lower, inverse, matrix, panels, mirrors, (rows_here, cols_here, sources, arrivals))


def solution(mesh):
    return jax.shard_map(
        body,
        mesh=mesh,
        in_specs=(P("row", "col"),),
        out_specs=P("row", "col"),
        check_vma=False,
    )
```

```python
import functools

import jax
import jax.numpy as jnp
from jax import lax
from jax.experimental import pallas as pl
from jax.experimental.pallas import tpu as pltpu
from jax.sharding import PartitionSpec as P

NB = 128
TILE = 256
AXES = ("row", "col")
HIGHEST = lax.Precision.HIGHEST
TRANS_B = (((1,), (1,)), ((), ()))


def factor_kernel(corner_ref, lower_ref, inverse_ref):
    works = lax.rem(lax.axis_index("row"), 2) == 0

    @pl.when(jnp.logical_not(works))
    def _():
        lower_ref[...] = jnp.zeros_like(lower_ref)
        inverse_ref[...] = jnp.zeros_like(inverse_ref)

    @pl.when(works)
    def _():
        eliminate(corner_ref, lower_ref, inverse_ref)


def eliminate(corner_ref, lower_ref, inverse_ref):
    blocks = NB // 8
    rows = lax.broadcasted_iota(jnp.int32, (NB, NB), 0)
    cols = lax.broadcasted_iota(jnp.int32, (NB, NB), 1)
    sub = lax.broadcasted_iota(jnp.int32, (8, NB), 0)
    corner = corner_ref[...]
    left = jnp.where(rows >= cols, corner, corner.T)
    right = jnp.where(rows == cols, 1.0, 0.0).astype(jnp.float32)
    lefts = [left[8 * b:8 * b + 8, :] for b in range(blocks)]
    rights = [right[8 * b:8 * b + 8, :] for b in range(blocks)]

    def whole(row):
        return jnp.broadcast_to(row, (8, NB))

    for b in range(blocks):
        def spread(i, b=b):
            return [jnp.broadcast_to(lefts[i][:, 8 * b + j:8 * b + j + 1], (8, NB)) for j in range(8)]

        here = spread(b)
        inverse_pivots, pivot_rows = [], []
        for k in range(8):
            inverse_pivots.append(1.0 / whole(here[k][k:k + 1, :]))
            pivot_rows.append([whole(column[k:k + 1, :]) for column in here])
            mult = jnp.where(sub > k, here[k] * inverse_pivots[k], 0.0)
            for j in range(k + 1, 8):
                here[j] = here[j] - mult * pivot_rows[k][j]
            lefts[b] = lefts[b] - mult * lefts[b][k:k + 1, :]
            rights[b] = rights[b] - mult * rights[b][k:k + 1, :]
        left_rows = [whole(lefts[b][k:k + 1, :]) for k in range(8)]
        right_rows = [whole(rights[b][k:k + 1, :]) for k in range(8)]
        for i in range(b + 1, blocks):
            there = spread(i)
            for k in range(8):
                mult = there[k] * inverse_pivots[k]
                for j in range(k + 1, 8):
                    there[j] = there[j] - mult * pivot_rows[k][j]
                lefts[i] = lefts[i] - mult * left_rows[k]
                rights[i] = rights[i] - mult * right_rows[k]
    upper = jnp.concatenate(lefts, axis=0)
    unit_inverse = jnp.concatenate(rights, axis=0)
    diagonal = jnp.sum(jnp.where(rows == cols, upper, 0.0), axis=1, keepdims=True)
    scale = 1.0 / jnp.sqrt(jnp.broadcast_to(diagonal, (NB, NB)))
    lower_ref[...] = jnp.where(rows >= cols, (upper * scale).T, 0.0)
    inverse_ref[...] = jnp.where(rows >= cols, unit_inverse * scale, 0.0)


def factor(corner):
    return pl.pallas_call(
        factor_kernel,
        out_shape=[jax.ShapeDtypeStruct((NB, NB), jnp.float32)] * 2,
        in_specs=[pl.BlockSpec(memory_space=pltpu.VMEM)],
        out_specs=[pl.BlockSpec(memory_space=pltpu.VMEM)] * 2,
        compiler_params=pltpu.CompilerParams(vmem_limit_bytes=4 * 1024 * 1024),
        cost_estimate=pl.CostEstimate(flops=4_000_000_000, bytes_accessed=40_000_000, transcendentals=0),
        name="factor",
    )(corner)


def split(value):
    high = value.astype(jnp.bfloat16)
    low = (value - high.astype(jnp.float32)).astype(jnp.bfloat16)
    return high, low


def update_kernel(plan, lower_ref, inverse_ref, inverse_from_ref, matrix_ref, panel_even_ref, panel_odd_ref,
                  mirror_even_ref, mirror_odd_ref, out_ref, old, new, panel, mirror, rhs, in_sems, panel_sems,
                  mirror_sems, out_sems):
    rows_here, cols_here, sources = plan
    row_index = lax.axis_index("row")
    col_index = lax.axis_index("col")
    height, width = old.shape
    col_blocks = width // NB
    each = mirror.shape[0] // sources
    tiles = height // TILE
    here = [pl.ds(i * TILE, TILE) for i in range(tiles)]
    odd = lax.rem(row_index, 2) == 1
    even = jnp.logical_not(odd)

    for q in range(sources):
        away = lax.rem(q - row_index // cols_here + sources, sources)
        for mirror_ref, here_if in [(mirror_odd_ref, odd), (mirror_even_ref, even)]:
            @pl.when(here_if)
            def _(q=q, away=away, mirror_ref=mirror_ref):
                source = mirror_ref.at[pl.ds(pl.multiple_of(away * each, each), each)]
                pltpu.make_async_copy(source, mirror.at[pl.ds(q * each, each)], mirror_sems.at[q]).start()

    first_column = matrix_ref.at[:, pl.ds(0, NB)]
    for i in range(tiles):
        for panel_ref, here_if in [(first_column, col_index == 0), (panel_odd_ref, odd & (col_index > 0)),
                                   (panel_even_ref, even & (col_index > 0))]:
            @pl.when(here_if)
            def _(i=i, panel_ref=panel_ref):
                pltpu.make_async_copy(panel_ref.at[here[i]], panel.at[here[i]], panel_sems.at[i]).start()
        pltpu.make_async_copy(matrix_ref.at[here[i]], old.at[here[i]], in_sems.at[i]).start()

    inverse = inverse_ref[...] + inverse_from_ref[...]
    for q in range(sources):
        half = pl.ds(q * each, each)
        pltpu.make_async_copy(mirror_odd_ref.at[half], mirror.at[half], mirror_sems.at[q]).wait()
    for t in range(col_blocks):
        block = (t % sources) * each + (t // sources) * NB
        part = lax.dot_general(inverse, mirror[pl.ds(block, NB), :], TRANS_B, precision=HIGHEST,
                               preferred_element_type=jnp.float32)
        high, low = split(part)
        at = pl.ds(t * NB, NB)
        rhs[pl.ds(0, NB), at] = high
        rhs[pl.ds(NB, NB), at] = high
        rhs[pl.ds(2 * NB, NB), at] = low

    for i in range(tiles):
        pltpu.make_async_copy(panel_odd_ref.at[here[i]], panel.at[here[i]], panel_sems.at[i]).wait()
        tall = lax.dot_general(panel[here[i], :], inverse, TRANS_B, precision=HIGHEST,
                               preferred_element_type=jnp.float32)
        high, low = split(tall)
        lhs = jnp.concatenate([high, low, high], axis=1)
        product = jnp.dot(lhs, rhs[...], preferred_element_type=jnp.float32)
        pltpu.make_async_copy(matrix_ref.at[here[i]], old.at[here[i]], in_sems.at[i]).wait()
        for s in range(TILE // NB):
            row = (i * (TILE // NB) + s) * rows_here + row_index
            down = pl.ds(i * TILE + s * NB, NB)
            for t in range(col_blocks):
                across = pl.ds(t * NB, NB)
                col = t * cols_here + col_index
                before = old[down, across]
                after = before - product[s * NB:(s + 1) * NB, t * NB:(t + 1) * NB]
                value = jnp.where((row >= col) & (col >= 1), after, before)
                if t == 0:
                    block = jnp.where(row == 0, lower_ref[...], tall[s * NB:(s + 1) * NB, :])
                    value = jnp.where(col == 0, block, value)
                new[down, across] = value
        pltpu.make_async_copy(new.at[here[i]], out_ref.at[here[i]], out_sems.at[i]).start()
    for i in range(tiles):
        pltpu.make_async_copy(new.at[here[i]], out_ref.at[here[i]], out_sems.at[i]).wait()


def update(lower, inverses, matrix, panels, mirrors, plan):
    height, width = matrix.shape
    sources = plan[2]
    tiles = height // TILE
    vmem = pl.BlockSpec(memory_space=pltpu.VMEM)
    anywhere = pl.BlockSpec(memory_space=pl.ANY)
    return pl.pallas_call(
        functools.partial(update_kernel, plan),
        out_shape=jax.ShapeDtypeStruct(matrix.shape, jnp.float32),
        in_specs=[vmem] * 3 + [pl.BlockSpec(memory_space=pltpu.HBM)] + [anywhere] * 4,
        out_specs=anywhere,
        scratch_shapes=[
            pltpu.VMEM((height, width), jnp.float32),
            pltpu.VMEM((height, width), jnp.float32),
            pltpu.VMEM((height, NB), jnp.float32),
            pltpu.VMEM((width, NB), jnp.float32),
            pltpu.VMEM((3 * NB, width), jnp.bfloat16),
            pltpu.SemaphoreType.DMA((tiles,)),
            pltpu.SemaphoreType.DMA((tiles,)),
            pltpu.SemaphoreType.DMA((sources,)),
            pltpu.SemaphoreType.DMA((tiles,)),
        ],
        compiler_params=pltpu.CompilerParams(vmem_limit_bytes=16 * 1024 * 1024),
        cost_estimate=pl.CostEstimate(flops=2 * height * width * NB * 3,
                                      bytes_accessed=8 * height * width, transcendentals=0),
        name="update",
    )(lower, *inverses, matrix, *panels, *mirrors)


def body(matrix):
    rows_here = lax.axis_size("row")
    cols_here = lax.axis_size("col")
    row_index = lax.axis_index("row")
    col_index = lax.axis_index("col")
    col_blocks = matrix.shape[1] // NB
    sources = rows_here // cols_here
    last = cols_here - 1
    even_rows = range(0, rows_here, 2)
    odd_rows = range(1, rows_here, 2)

    def send(value, pairs):
        return lax.ppermute(value, AXES, [(a * cols_here + b, c * cols_here + d) for (a, b), (c, d) in pairs])

    def after(value, *others):
        return lax.optimization_barrier((value, *others))[0]

    corner = jnp.where((row_index == 0) & (col_index == 0), matrix[:NB, :NB], 0.0)
    corner = corner + send(corner, [((0, 0), (0, last))])
    crossed = corner
    holders = [(0, last)]
    hops = [(1 << b, 0) for b in reversed(range(1, rows_here.bit_length() - 1))]
    hops += [(0, 1 << b) for b in range(cols_here.bit_length() - 1)]
    for dr, dc in hops:
        moved = [(r + dr, c - dc) for r, c in holders]
        corner = corner + send(corner, [(h, m) for h, m in zip(holders, moved) if m != (0, 0)])
        holders = holders + moved

    column = after(matrix[:, :NB], crossed)
    even_panel = send(column, [((r, 0), (r + 1, 0)) for r in even_rows])
    odd_panel = jnp.where(col_index == 0, after(column, even_panel), 0.0)

    half = NB * (col_blocks // sources)
    of_odd = send(odd_panel[:half], [((r, 0), (r, r % cols_here)) for r in odd_rows])
    of_even = send(even_panel[:half], [((r, 0), (r, (r - 1) % cols_here)) for r in odd_rows if (r - 1) % cols_here])
    keeps = (col_index == 0) & (row_index % cols_here == 1)
    mirror = of_odd + of_even + jnp.where(keeps, even_panel[:half], 0.0)
    holders = [((c + q * cols_here) | 1, c) for c in range(cols_here) for q in range(sources)]
    for bit in (1 << b for b in range(1, cols_here.bit_length() - 1)):
        moved = [(r ^ bit, c) for r, c in holders]
        mirror = mirror + send(mirror, list(zip(holders, moved)))
        holders = holders + moved
    mirror = jnp.concatenate([mirror] + [
        send(mirror, [(((r + q * cols_here) % rows_here, c), (r, c)) for r, c in holders])
        for q in range(1, sources)], axis=0)

    step = 1
    while step < cols_here:
        base = [(r, c) for r in odd_rows for c in range(step)]
        near = [((r, c), (r, c + step)) for r, c in base]
        far = [((r, c), (r, c + 2 * step)) for r, c in base]
        near_last = [((r, c + step), (r, c + 3 * step)) for r, c in base]
        far_last = [((r, c + 2 * step), (r, c + 3 * step)) for r, c in base]
        odd_first = odd_panel + send(odd_panel, near)
        even_first = even_panel + send(even_panel, far)
        odd_second = send(odd_first, far + near_last)
        even_second = send(even_first, near + far_last)
        odd_panel = odd_first + odd_second
        even_panel = even_first + even_second
        step *= 4

    lower, inverse = factor(corner)

    down = [((r, c), (r - 1, c)) for r in odd_rows for c in range(cols_here)]
    panel = send(even_panel, down)
    mirrors = [send(mirror, down), mirror]
    inverses = [inverse, send(inverse, [(b, a) for a, b in down])]
    return update(lower, inverses, matrix, [panel, odd_panel], mirrors, (rows_here, cols_here, sources))


def solution(mesh):
    return jax.shard_map(
        body,
        mesh=mesh,
        in_specs=(P("row", "col"),),
        out_specs=P("row", "col"),
        check_vma=False,
    )
```

```python
import functools

import jax
import jax.numpy as jnp
from jax import lax
from jax.experimental import pallas as pl
from jax.experimental.pallas import tpu as pltpu
from jax.sharding import PartitionSpec as P

NB = 128
TILE = 256
AXES = ("row", "col")
HIGHEST = lax.Precision.HIGHEST
TRANS_B = (((1,), (1,)), ((), ()))


def factor_kernel(matrix_ref, lower_ref, inverse_ref, corner_ref, sem):
    works = (lax.axis_index("row") == 0) & (lax.axis_index("col") == 0)

    @pl.when(jnp.logical_not(works))
    def _():
        lower_ref[...] = jnp.zeros_like(lower_ref)
        inverse_ref[...] = jnp.zeros_like(inverse_ref)

    @pl.when(works)
    def _():
        copy = pltpu.make_async_copy(matrix_ref.at[pl.ds(0, NB), pl.ds(0, NB)], corner_ref, sem)
        copy.start()
        copy.wait()
        eliminate(corner_ref, lower_ref, inverse_ref)


def eliminate(corner_ref, lower_ref, inverse_ref):
    blocks = NB // 8
    rows = lax.broadcasted_iota(jnp.int32, (NB, NB), 0)
    cols = lax.broadcasted_iota(jnp.int32, (NB, NB), 1)
    sub = lax.broadcasted_iota(jnp.int32, (8, NB), 0)
    corner = corner_ref[...]
    left = jnp.where(rows >= cols, corner, corner.T)
    right = jnp.where(rows == cols, 1.0, 0.0).astype(jnp.float32)
    lefts = [left[8 * b:8 * b + 8, :] for b in range(blocks)]
    rights = [right[8 * b:8 * b + 8, :] for b in range(blocks)]

    def whole(row):
        return jnp.broadcast_to(row, (8, NB))

    for b in range(blocks):
        def spread(i, b=b):
            return [jnp.broadcast_to(lefts[i][:, 8 * b + j:8 * b + j + 1], (8, NB)) for j in range(8)]

        here = spread(b)
        inverse_pivots, pivot_rows = [], []
        for k in range(8):
            inverse_pivots.append(1.0 / whole(here[k][k:k + 1, :]))
            pivot_rows.append([whole(column[k:k + 1, :]) for column in here])
            mult = jnp.where(sub > k, here[k] * inverse_pivots[k], 0.0)
            for j in range(k + 1, 8):
                here[j] = here[j] - mult * pivot_rows[k][j]
            lefts[b] = lefts[b] - mult * lefts[b][k:k + 1, :]
            rights[b] = rights[b] - mult * rights[b][k:k + 1, :]
        left_rows = [whole(lefts[b][k:k + 1, :]) for k in range(8)]
        right_rows = [whole(rights[b][k:k + 1, :]) for k in range(8)]
        for i in range(b + 1, blocks):
            there = spread(i)
            for k in range(8):
                mult = there[k] * inverse_pivots[k]
                for j in range(k + 1, 8):
                    there[j] = there[j] - mult * pivot_rows[k][j]
                lefts[i] = lefts[i] - mult * left_rows[k]
                rights[i] = rights[i] - mult * right_rows[k]
    upper = jnp.concatenate(lefts, axis=0)
    unit_inverse = jnp.concatenate(rights, axis=0)
    diagonal = jnp.sum(jnp.where(rows == cols, upper, 0.0), axis=1, keepdims=True)
    scale = 1.0 / jnp.sqrt(jnp.broadcast_to(diagonal, (NB, NB)))
    lower_ref[...] = jnp.where(rows >= cols, (upper * scale).T, 0.0)
    inverse_ref[...] = jnp.where(rows >= cols, unit_inverse * scale, 0.0)


def factor(matrix):
    return pl.pallas_call(
        factor_kernel,
        out_shape=[jax.ShapeDtypeStruct((NB, NB), jnp.float32)] * 2,
        in_specs=[pl.BlockSpec(memory_space=pltpu.HBM)],
        out_specs=[pl.BlockSpec(memory_space=pltpu.VMEM)] * 2,
        scratch_shapes=[pltpu.VMEM((NB, NB), jnp.float32), pltpu.SemaphoreType.DMA],
        compiler_params=pltpu.CompilerParams(vmem_limit_bytes=62 * 1024 * 1024),
        cost_estimate=pl.CostEstimate(flops=4_000_000, bytes_accessed=200_000, transcendentals=0),
        name="factor",
    )(matrix)


def split(value):
    high = value.astype(jnp.bfloat16)
    low = (value - high.astype(jnp.float32)).astype(jnp.bfloat16)
    return high, low


def update_kernel(plan, lower_ref, inverse_ref, inverse_from_ref, matrix_ref, mirror_even_ref, mirror_odd_ref, *refs):
    rows_here, cols_here, sources = plan
    panel_refs = refs[:cols_here - 1]
    out_ref, new, panel, mirror, rhs, out_sems = refs[cols_here - 1:]
    row_index = lax.axis_index("row")
    col_index = lax.axis_index("col")
    height, width = matrix_ref.shape
    col_blocks = width // NB
    each = mirror.shape[0] // sources
    tiles = height // TILE
    here = [pl.ds(i * TILE, TILE) for i in range(tiles)]
    odd = lax.rem(row_index, 2) == 1

    for q in range(sources):
        away = lax.rem(q - row_index // cols_here + sources, sources)
        for mirror_ref, here_if in [(mirror_odd_ref, odd), (mirror_even_ref, jnp.logical_not(odd))]:
            @pl.when(here_if)
            def _(q=q, away=away, mirror_ref=mirror_ref):
                mirror[pl.ds(q * each, each), :] = mirror_ref[pl.ds(pl.multiple_of(away * each, each), each), :]

    @pl.when(col_index == 0)
    def _():
        panel[...] = matrix_ref[:, pl.ds(0, NB)]

    for c in range(1, cols_here):
        @pl.when(col_index == c)
        def _(c=c):
            panel[...] = panel_refs[c - 1][...]

    inverse = inverse_ref[...] + inverse_from_ref[...]
    for t in range(col_blocks):
        block = (t % sources) * each + (t // sources) * NB
        part = lax.dot_general(inverse, mirror[pl.ds(block, NB), :], TRANS_B, precision=HIGHEST,
                               preferred_element_type=jnp.float32)
        high, low = split(part)
        at = pl.ds(t * NB, NB)
        rhs[pl.ds(0, NB), at] = high
        rhs[pl.ds(NB, NB), at] = high
        rhs[pl.ds(2 * NB, NB), at] = low

    for i in range(tiles):
        tall = lax.dot_general(panel[here[i], :], inverse, TRANS_B, precision=HIGHEST,
                               preferred_element_type=jnp.float32)
        high, low = split(tall)
        lhs = jnp.concatenate([high, low, high], axis=1)
        product = jnp.dot(lhs, rhs[...], preferred_element_type=jnp.float32)
        for s in range(TILE // NB):
            row = (i * (TILE // NB) + s) * rows_here + row_index
            down = pl.ds(i * TILE + s * NB, NB)
            for t in range(col_blocks):
                across = pl.ds(t * NB, NB)
                col = t * cols_here + col_index
                before = matrix_ref[down, across]
                after = before - product[s * NB:(s + 1) * NB, t * NB:(t + 1) * NB]
                value = jnp.where((row >= col) & (col >= 1), after, before)
                if t == 0:
                    block = tall[s * NB:(s + 1) * NB, :]
                    if i == 0 and s == 0:
                        block = jnp.where(row == 0, lower_ref[...], block)
                    value = jnp.where(col == 0, block, value)
                new[down, across] = value
        pltpu.make_async_copy(new.at[here[i]], out_ref.at[here[i]], out_sems.at[i]).start()
    for i in range(tiles):
        pltpu.make_async_copy(new.at[here[i]], out_ref.at[here[i]], out_sems.at[i]).wait()


def update(lower, inverses, matrix, panels, mirrors, plan):
    height, width = matrix.shape
    tiles = height // TILE
    vmem = pl.BlockSpec(memory_space=pltpu.VMEM)
    return pl.pallas_call(
        functools.partial(update_kernel, plan),
        out_shape=jax.ShapeDtypeStruct(matrix.shape, jnp.float32),
        in_specs=[vmem] * (4 + len(mirrors) + len(panels)),
        out_specs=pl.BlockSpec(memory_space=pl.ANY),
        scratch_shapes=[
            pltpu.VMEM((height, width), jnp.float32),
            pltpu.VMEM((height, NB), jnp.float32),
            pltpu.VMEM((width, NB), jnp.float32),
            pltpu.VMEM((3 * NB, width), jnp.bfloat16),
            pltpu.SemaphoreType.DMA((tiles,)),
        ],
        compiler_params=pltpu.CompilerParams(vmem_limit_bytes=28 * 1024 * 1024),
        cost_estimate=pl.CostEstimate(flops=2 * height * width * NB * 3,
                                      bytes_accessed=8 * height * width, transcendentals=0),
        name="update",
    )(lower, *inverses, matrix, *mirrors, *panels)


TIES = {'mode': 'Y', 'A': 0, 'E1': 0, 'E2': 0, 'E3': None, 'M1': 1, 'M2': 3, 'X1': 4, 'need': {4: [1, 2]}, 'X1need': False}


def body(matrix):
    rows_here = lax.axis_size("row")
    cols_here = lax.axis_size("col")
    row_index = lax.axis_index("row")
    col_index = lax.axis_index("col")
    col_blocks = matrix.shape[1] // NB
    sources = rows_here // cols_here
    last = cols_here - 1
    every_row = range(rows_here)
    even_rows = range(0, rows_here, 2)
    odd_rows = range(1, rows_here, 2)
    T = TIES

    def send(value, pairs):
        return lax.ppermute(value, AXES, [(a * cols_here + b, c * cols_here + d) for (a, b), (c, d) in pairs])

    def after(value, *others):
        return lax.optimization_barrier((value, *others))[0]

    column = matrix[:, :NB]
    half = NB * (col_blocks // sources)
    first = column[:half]
    if T["mode"] == "Y":
        lower, inverse = factor(matrix)
    else:
        inverse = jnp.where((row_index == 0) & (col_index == 0), matrix[:NB, :NB], 0.0)
    inverse = inverse + send(inverse, [((0, 0), (0, last))])
    along = [inverse]
    bulk = {}

    def tie(value, name):
        t = T[name]
        return value if t is None or t >= len(along) else after(value, along[t])

    def try_bulk():
        if "A" not in bulk and T["A"] < len(along):
            bulk["A"] = send(tie(first, "A"), [((r, 0), (r | 1, r % cols_here)) for r in every_row])
        if 1 not in bulk and T["E1"] < len(along):
            merged = tie(column, "E1")
            step = 1
            while step < cols_here:
                base = [(r, c) for r in every_row for c in range(step)]
                near = send(merged, [((r, c), (r, c + step)) for r, c in base])
                far = send(merged, [((r, c), (r, c + 2 * step)) for r, c in base])
                both = near + far
                if T["E3"] is not None and T["E3"] < len(along): both = after(both, along[T["E3"]])
                relay = send(both, [((r, c + step * (1 + r % 2)), (r, c + 3 * step)) for r, c in base])
                for c in range(step):
                    bulk[c + step], bulk[c + 2 * step], bulk[c + 3 * step] = near, far, relay
                step *= 4
                if step < cols_here:
                    merged = jnp.where(col_index == 0, column, 0.0) + sum({id(v): v for k, v in bulk.items() if k != "A"}.values())

    holders = [(0, last)]
    hops = [(1 << b, 0) for b in reversed(range(1, rows_here.bit_length() - 1))]
    hops += [(0, 1 << b) for b in range(cols_here.bit_length() - 1)]
    for n, (dr, dc) in enumerate(hops):
        try_bulk()
        need = [bulk[k] for k in T["need"].get(n + 1, []) if k in bulk]
        if need:
            inverse, *got = lax.optimization_barrier((inverse, *need))
            for k, v in zip([k for k in T["need"][n + 1] if k in bulk], got): bulk[k] = v
        moved = [(r + dr, c - dc) for r, c in holders]
        inverse = inverse + send(inverse, [(h, m) for h, m in zip(holders, moved) if m != (0, 0)])
        holders = holders + moved
        along.append(inverse)
    try_bulk()
    panels = [bulk[c] for c in range(1, cols_here)]

    mirror = bulk["A"]
    holders = [((c + q * cols_here) | 1, c) for c in range(cols_here) for q in range(sources)]
    mirror = tie(mirror, "M1")
    for bit in (1 << b for b in range(1, cols_here.bit_length() - 1)):
        moved = [(r ^ bit, c) for r, c in holders]
        mirror = mirror + send(mirror, list(zip(holders, moved)))
        holders = holders + moved
    mirror = tie(mirror, "M2")
    mirror = jnp.concatenate([mirror] + [
        send(mirror, [(((r + q * cols_here) % rows_here, c), (r, c)) for r, c in holders])
        for q in range(1, sources)], axis=0)
    need = T["need"].get(5, [])
    if need:
        inverse, *got = lax.optimization_barrier((inverse, *[panels[k - 1] for k in need]))
        for k, v in zip(need, got): panels[k - 1] = v
    if T.get("X1need"):
        mirror, *panels = lax.optimization_barrier((mirror, *panels))
    mirror = tie(mirror, "X1")
    if T["mode"] == "X":
        lower, inverse = factor(inverse)
    down = [((r, c), (r - 1, c)) for r in odd_rows for c in range(cols_here)]
    mirrors = [send(mirror, down), mirror]
    inverses = [inverse, send(inverse, [(b, a) for a, b in down])]
    return update(lower, inverses, matrix, panels, mirrors, (rows_here, cols_here, sources))


def solution(mesh):
    return jax.shard_map(
        body,
        mesh=mesh,
        in_specs=(P("row", "col"),),
        out_specs=P("row", "col"),
        check_vma=False,
    )
```

```python
import functools

import jax
import jax.numpy as jnp
from jax import lax
from jax.experimental import pallas as pl
from jax.experimental.pallas import tpu as pltpu
from jax.sharding import PartitionSpec as P

NB = 128
TILE = 256
AXES = ("row", "col")
HIGHEST = lax.Precision.HIGHEST
TRANS_B = (((1,), (1,)), ((), ()))


def factor_kernel(matrix_ref, lower_ref, inverse_ref, column_ref, half_ref, corner_ref, sems):
    works = (lax.axis_index("row") == 0) & (lax.axis_index("col") == 0)
    first = pl.ds(0, NB)
    copies = [
        pltpu.make_async_copy(matrix_ref.at[first, first], corner_ref, sems.at[0]),
        pltpu.make_async_copy(matrix_ref.at[pl.ds(0, half_ref.shape[0]), first], half_ref, sems.at[1]),
        pltpu.make_async_copy(matrix_ref.at[:, first], column_ref, sems.at[2]),
    ]
    for copy in copies:
        copy.start()
    copies[0].wait()

    @pl.when(works)
    def _():
        eliminate(corner_ref, lower_ref, inverse_ref)

    for copy in copies[1:]:
        copy.wait()


def eliminate(corner_ref, lower_ref, inverse_ref):
    blocks = NB // 8
    rows = lax.broadcasted_iota(jnp.int32, (NB, NB), 0)
    cols = lax.broadcasted_iota(jnp.int32, (NB, NB), 1)
    sub = lax.broadcasted_iota(jnp.int32, (8, NB), 0)
    corner = corner_ref[...]
    left = jnp.where(rows >= cols, corner, corner.T)
    right = jnp.where(rows == cols, 1.0, 0.0).astype(jnp.float32)
    lefts = [left[8 * b:8 * b + 8, :] for b in range(blocks)]
    rights = [right[8 * b:8 * b + 8, :] for b in range(blocks)]

    def whole(row):
        return jnp.broadcast_to(row, (8, NB))

    for b in range(blocks):
        def spread(i, b=b):
            return [jnp.broadcast_to(lefts[i][:, 8 * b + j:8 * b + j + 1], (8, NB)) for j in range(8)]

        here = spread(b)
        inverse_pivots, pivot_rows = [], []
        for k in range(8):
            inverse_pivots.append(1.0 / whole(here[k][k:k + 1, :]))
            pivot_rows.append([whole(column[k:k + 1, :]) for column in here])
            mult = jnp.where(sub > k, here[k] * inverse_pivots[k], 0.0)
            for j in range(k + 1, 8):
                here[j] = here[j] - mult * pivot_rows[k][j]
            lefts[b] = lefts[b] - mult * lefts[b][k:k + 1, :]
            rights[b] = rights[b] - mult * rights[b][k:k + 1, :]
        left_rows = [whole(lefts[b][k:k + 1, :]) for k in range(8)]
        right_rows = [whole(rights[b][k:k + 1, :]) for k in range(8)]
        for i in range(b + 1, blocks):
            there = spread(i)
            for k in range(8):
                mult = there[k] * inverse_pivots[k]
                for j in range(k + 1, 8):
                    there[j] = there[j] - mult * pivot_rows[k][j]
                lefts[i] = lefts[i] - mult * left_rows[k]
                rights[i] = rights[i] - mult * right_rows[k]
    upper = jnp.concatenate(lefts, axis=0)
    unit_inverse = jnp.concatenate(rights, axis=0)
    diagonal = jnp.sum(jnp.where(rows == cols, upper, 0.0), axis=1, keepdims=True)
    scale = 1.0 / jnp.sqrt(jnp.broadcast_to(diagonal, (NB, NB)))
    lower_ref[...] = jnp.where(rows >= cols, (upper * scale).T, 0.0)
    inverse_ref[...] = jnp.where(rows >= cols, unit_inverse * scale, 0.0)


def factor(matrix, half):
    square = jax.ShapeDtypeStruct((NB, NB), jnp.float32)
    tall = [jax.ShapeDtypeStruct((rows, NB), jnp.float32) for rows in (matrix.shape[0], half)]
    return pl.pallas_call(
        factor_kernel,
        out_shape=[square, square, *tall],
        in_specs=[pl.BlockSpec(memory_space=pltpu.HBM)],
        out_specs=[pl.BlockSpec(memory_space=pltpu.VMEM)] * 2 + [pl.BlockSpec(memory_space=pltpu.VMEM)] * 2,
        scratch_shapes=[pltpu.VMEM((NB, NB), jnp.float32), pltpu.SemaphoreType.DMA((3,))],
        compiler_params=pltpu.CompilerParams(vmem_limit_bytes=62 * 1024 * 1024),
        cost_estimate=pl.CostEstimate(flops=4_000_000, bytes_accessed=200_000, transcendentals=0),
        name="factor",
    )(matrix)


def split(value):
    high = value.astype(jnp.bfloat16)
    low = (value - high.astype(jnp.float32)).astype(jnp.bfloat16)
    return high, low


def update_kernel(plan, lower_ref, inverse_ref, inverse_from_ref, matrix_ref, mirror_even_ref, mirror_odd_ref, *refs):
    rows_here, cols_here, sources = plan
    panel_refs = refs[:cols_here - 1]
    out_ref, new, panel, mirror, rhs, out_sems = refs[cols_here - 1:]
    row_index = lax.axis_index("row")
    col_index = lax.axis_index("col")
    height, width = matrix_ref.shape
    col_blocks = width // NB
    each = mirror.shape[0] // sources
    tiles = height // TILE
    here = [pl.ds(i * TILE, TILE) for i in range(tiles)]
    odd = lax.rem(row_index, 2) == 1

    for q in range(sources):
        away = lax.rem(q - row_index // cols_here + sources, sources)
        for mirror_ref, here_if in [(mirror_odd_ref, odd), (mirror_even_ref, jnp.logical_not(odd))]:
            @pl.when(here_if)
            def _(q=q, away=away, mirror_ref=mirror_ref):
                mirror[pl.ds(q * each, each), :] = mirror_ref[pl.ds(pl.multiple_of(away * each, each), each), :]

    @pl.when(col_index == 0)
    def _():
        panel[...] = matrix_ref[:, pl.ds(0, NB)]

    for c in range(1, cols_here):
        @pl.when(col_index == c)
        def _(c=c):
            panel[...] = panel_refs[c - 1][...]

    inverse = inverse_ref[...] + inverse_from_ref[...]
    for t in range(col_blocks):
        block = (t % sources) * each + (t // sources) * NB
        part = lax.dot_general(inverse, mirror[pl.ds(block, NB), :], TRANS_B, precision=HIGHEST,
                               preferred_element_type=jnp.float32)
        high, low = split(part)
        at = pl.ds(t * NB, NB)
        rhs[pl.ds(0, NB), at] = high
        rhs[pl.ds(NB, NB), at] = high
        rhs[pl.ds(2 * NB, NB), at] = low

    for i in range(tiles):
        tall = lax.dot_general(panel[here[i], :], inverse, TRANS_B, precision=HIGHEST,
                               preferred_element_type=jnp.float32)
        high, low = split(tall)
        lhs = jnp.concatenate([high, low, high], axis=1)
        product = jnp.dot(lhs, rhs[...], preferred_element_type=jnp.float32)
        for s in range(TILE // NB):
            row = (i * (TILE // NB) + s) * rows_here + row_index
            down = pl.ds(i * TILE + s * NB, NB)
            for t in range(col_blocks):
                across = pl.ds(t * NB, NB)
                col = t * cols_here + col_index
                before = matrix_ref[down, across]
                after = before - product[s * NB:(s + 1) * NB, t * NB:(t + 1) * NB]
                value = jnp.where((row >= col) & (col >= 1), after, before)
                if t == 0:
                    block = tall[s * NB:(s + 1) * NB, :]
                    if i == 0 and s == 0:
                        block = jnp.where(row == 0, lower_ref[...], block)
                    value = jnp.where(col == 0, block, value)
                new[down, across] = value
        pltpu.make_async_copy(new.at[here[i]], out_ref.at[here[i]], out_sems.at[i]).start()
    for i in range(tiles):
        pltpu.make_async_copy(new.at[here[i]], out_ref.at[here[i]], out_sems.at[i]).wait()


def update(lower, inverses, matrix, panels, mirrors, plan):
    height, width = matrix.shape
    tiles = height // TILE
    vmem = pl.BlockSpec(memory_space=pltpu.VMEM)
    return pl.pallas_call(
        functools.partial(update_kernel, plan),
        out_shape=jax.ShapeDtypeStruct(matrix.shape, jnp.float32),
        in_specs=[vmem] * (4 + len(mirrors) + len(panels)),
        out_specs=pl.BlockSpec(memory_space=pl.ANY),
        scratch_shapes=[
            pltpu.VMEM((height, width), jnp.float32),
            pltpu.VMEM((height, NB), jnp.float32),
            pltpu.VMEM((width, NB), jnp.float32),
            pltpu.VMEM((3 * NB, width), jnp.bfloat16),
            pltpu.SemaphoreType.DMA((tiles,)),
        ],
        compiler_params=pltpu.CompilerParams(vmem_limit_bytes=28 * 1024 * 1024),
        cost_estimate=pl.CostEstimate(flops=2 * height * width * NB * 3,
                                      bytes_accessed=8 * height * width, transcendentals=0),
        name="update",
    )(lower, *inverses, matrix, *mirrors, *panels)

def body(matrix):
    rows_here = lax.axis_size("row")
    cols_here = lax.axis_size("col")
    row_index = lax.axis_index("row")
    col_index = lax.axis_index("col")
    sources = rows_here // cols_here
    every_row = range(rows_here)
    odd_rows = range(1, rows_here, 2)
    last = cols_here - 1

    def send(value, pairs):
        return lax.ppermute(value, AXES, [(a * cols_here + b, c * cols_here + d) for (a, b), (c, d) in pairs])

    lower, inverse, column, first = factor(matrix, matrix.shape[1] // sources)
    lower = jnp.where((row_index == 0) & (col_index == 0), lower, 0.0)

    mirror = send(first, [((r, 0), (r | 1, r % cols_here)) for r in every_row])

    panels = [None] * last
    straight = []
    merged = column
    step = 1
    while step < cols_here:
        base = [(r, c) for r in every_row for c in range(step)]
        near = send(merged, [((r, c), (r, c + step)) for r, c in base])
        far = send(merged, [((r, c), (r, c + 2 * step)) for r, c in base])
        relayed = send(near + far, [((r, c + step * (1 + r % 2)), (r, c + 3 * step)) for r, c in base])
        straight += [near, far]
        for c in range(step):
            panels[c + step - 1], panels[c + 2 * step - 1], panels[c + 3 * step - 1] = near, far, relayed
        merged = merged + near + far + relayed if step > 1 else (
            jnp.where(col_index == 0, column, 0.0) + near + far + relayed)
        step *= 4

    inverse = send(inverse, [((0, 0), (0, last))])
    holders = [(0, last)]
    hops = [(1 << b, 0) for b in reversed(range(1, rows_here.bit_length() - 1))]
    hops += [(0, 1 << b) for b in range(cols_here.bit_length() - 1)]
    along = [inverse]
    for dr, dc in hops:
        if len(along) == len(hops):
            inverse = lax.optimization_barrier((inverse, *straight))[0]
        moved = [(r + dr, c - dc) for r, c in holders]
        inverse = inverse + send(inverse, list(zip(holders, moved)))
        holders = holders + moved
        along.append(inverse)

    mirror, lower = lax.optimization_barrier((mirror, lower, along[1]))[:2]
    holders = [((c + q * cols_here) | 1, c) for c in range(cols_here) for q in range(sources)]
    for bit in (1 << b for b in range(1, cols_here.bit_length() - 1)):
        moved = [(r ^ bit, c) for r, c in holders]
        mirror = mirror + send(mirror, list(zip(holders, moved)))
        holders = holders + moved
    mirror = lax.optimization_barrier((mirror, along[-2]))[0]
    mirror = jnp.concatenate([mirror] + [
        send(mirror, [(((r + q * cols_here) % rows_here, c), (r, c)) for r, c in holders])
        for q in range(1, sources)], axis=0)
    mirror = lax.optimization_barrier((mirror, inverse))[0]

    down = [((r, c), (r - 1, c)) for r in odd_rows for c in range(cols_here)]
    mirrors = [send(mirror, down), mirror]
    inverses = [inverse, send(inverse, [(b, a) for a, b in down])]
    return update(lower, inverses, matrix, panels, mirrors, (rows_here, cols_here, sources))


def solution(mesh):
    return jax.shard_map(
        body,
        mesh=mesh,
        in_specs=(P("row", "col"),),
        out_specs=P("row", "col"),
        check_vma=False,
    )
```

```python
import functools

import jax
import jax.numpy as jnp
from jax import lax
from jax.experimental import pallas as pl
from jax.experimental.pallas import tpu as pltpu
from jax.sharding import PartitionSpec as P

NB = 128
TILE = 256
AXES = ("row", "col")
HIGHEST = lax.Precision.HIGHEST
TRANS_B = (((1,), (1,)), ((), ()))


def factor_kernel(matrix_ref, lower_ref, inverse_ref, column_ref, half_ref, corner_ref, sems):
    works = (lax.axis_index("row") == 0) & (lax.axis_index("col") == 0)
    first = pl.ds(0, NB)
    copies = [
        pltpu.make_async_copy(matrix_ref.at[first, first], corner_ref, sems.at[0]),
        pltpu.make_async_copy(matrix_ref.at[pl.ds(0, half_ref.shape[0]), first], half_ref, sems.at[1]),
        pltpu.make_async_copy(matrix_ref.at[:, first], column_ref, sems.at[2]),
    ]
    for copy in copies:
        copy.start()
    copies[0].wait()

    @pl.when(works)
    def _():
        eliminate(corner_ref, lower_ref, inverse_ref)

    for copy in copies[1:]:
        copy.wait()


def eliminate(corner_ref, lower_ref, inverse_ref):
    blocks = NB // 8
    rows = lax.broadcasted_iota(jnp.int32, (NB, NB), 0)
    cols = lax.broadcasted_iota(jnp.int32, (NB, NB), 1)
    sub = lax.broadcasted_iota(jnp.int32, (8, NB), 0)
    corner = corner_ref[...]
    left = jnp.where(rows >= cols, corner, corner.T)
    right = jnp.where(rows == cols, 1.0, 0.0).astype(jnp.float32)
    lefts = [left[8 * b:8 * b + 8, :] for b in range(blocks)]
    rights = [right[8 * b:8 * b + 8, :] for b in range(blocks)]

    def whole(row):
        return jnp.broadcast_to(row, (8, NB))

    for b in range(blocks):
        def spread(i, b=b):
            return [jnp.broadcast_to(lefts[i][:, 8 * b + j:8 * b + j + 1], (8, NB)) for j in range(8)]

        here = spread(b)
        inverse_pivots, pivot_rows = [], []
        for k in range(8):
            inverse_pivots.append(1.0 / whole(here[k][k:k + 1, :]))
            pivot_rows.append([whole(column[k:k + 1, :]) for column in here])
            mult = jnp.where(sub > k, here[k] * inverse_pivots[k], 0.0)
            for j in range(k + 1, 8):
                here[j] = here[j] - mult * pivot_rows[k][j]
            lefts[b] = lefts[b] - mult * lefts[b][k:k + 1, :]
            rights[b] = rights[b] - mult * rights[b][k:k + 1, :]
        left_rows = [whole(lefts[b][k:k + 1, :]) for k in range(8)]
        right_rows = [whole(rights[b][k:k + 1, :]) for k in range(8)]
        for i in range(b + 1, blocks):
            there = spread(i)
            for k in range(8):
                mult = there[k] * inverse_pivots[k]
                for j in range(k + 1, 8):
                    there[j] = there[j] - mult * pivot_rows[k][j]
                lefts[i] = lefts[i] - mult * left_rows[k]
                rights[i] = rights[i] - mult * right_rows[k]
    upper = jnp.concatenate(lefts, axis=0)
    unit_inverse = jnp.concatenate(rights, axis=0)
    diagonal = jnp.sum(jnp.where(rows == cols, upper, 0.0), axis=1, keepdims=True)
    scale = 1.0 / jnp.sqrt(jnp.broadcast_to(diagonal, (NB, NB)))
    lower_ref[...] = jnp.where(rows >= cols, (upper * scale).T, 0.0)
    inverse_ref[...] = jnp.where(rows >= cols, unit_inverse * scale, 0.0)


def factor(matrix, half):
    square = jax.ShapeDtypeStruct((NB, NB), jnp.float32)
    tall = [jax.ShapeDtypeStruct((rows, NB), jnp.float32) for rows in (matrix.shape[0], half)]
    return pl.pallas_call(
        factor_kernel,
        out_shape=[square, square, *tall],
        in_specs=[pl.BlockSpec(memory_space=pltpu.HBM)],
        out_specs=[pl.BlockSpec(memory_space=pltpu.VMEM)] * 2 + [pl.BlockSpec(memory_space=pltpu.VMEM)] * 2,
        scratch_shapes=[pltpu.VMEM((NB, NB), jnp.float32), pltpu.SemaphoreType.DMA((3,))],
        compiler_params=pltpu.CompilerParams(vmem_limit_bytes=62 * 1024 * 1024),
        cost_estimate=pl.CostEstimate(flops=4_000_000, bytes_accessed=200_000, transcendentals=0),
        name="factor",
    )(matrix)


def split(value):
    high = value.astype(jnp.bfloat16)
    low = (value - high.astype(jnp.float32)).astype(jnp.bfloat16)
    return high, low


def update_kernel(plan, lower_ref, inverse_ref, inverse_from_ref, matrix_ref, mirror_even_ref, mirror_odd_ref, *refs):
    rows_here, cols_here, sources = plan
    panel_refs = refs[:cols_here - 1]
    out_ref, new, panel, mirror, rhs, out_sems = refs[cols_here - 1:]
    row_index = lax.axis_index("row")
    col_index = lax.axis_index("col")
    height, width = matrix_ref.shape
    col_blocks = width // NB
    each = mirror.shape[0] // sources
    tiles = height // TILE
    here = [pl.ds(i * TILE, TILE) for i in range(tiles)]
    odd = lax.rem(row_index, 2) == 1

    for q in range(sources):
        away = lax.rem(q - row_index // cols_here + sources, sources)
        for mirror_ref, here_if in [(mirror_odd_ref, odd), (mirror_even_ref, jnp.logical_not(odd))]:
            @pl.when(here_if)
            def _(q=q, away=away, mirror_ref=mirror_ref):
                mirror[pl.ds(q * each, each), :] = mirror_ref[pl.ds(pl.multiple_of(away * each, each), each), :]

    @pl.when(col_index == 0)
    def _():
        panel[...] = matrix_ref[:, pl.ds(0, NB)]

    for c in range(1, cols_here):
        @pl.when(col_index == c)
        def _(c=c):
            panel[...] = panel_refs[c - 1][...]

    inverse = inverse_ref[...] + inverse_from_ref[...]
    for t in range(col_blocks):
        block = (t % sources) * each + (t // sources) * NB
        part = lax.dot_general(mirror[pl.ds(block, NB), :], inverse, TRANS_B, precision=HIGHEST,
                               preferred_element_type=jnp.float32)
        high, low = split(part)
        at = pl.ds(t * NB, NB)
        rhs[at, pl.ds(0, NB)] = high
        rhs[at, pl.ds(NB, NB)] = high
        rhs[at, pl.ds(2 * NB, NB)] = low

    for i in range(tiles):
        tall = lax.dot_general(panel[here[i], :], inverse, TRANS_B, precision=HIGHEST,
                               preferred_element_type=jnp.float32)
        high, low = split(tall)
        lhs = jnp.concatenate([high, low, high], axis=1)
        product = lax.dot_general(lhs, rhs[...], TRANS_B, preferred_element_type=jnp.float32)
        for s in range(TILE // NB):
            row = (i * (TILE // NB) + s) * rows_here + row_index
            down = pl.ds(i * TILE + s * NB, NB)
            for t in range(col_blocks):
                across = pl.ds(t * NB, NB)
                col = t * cols_here + col_index
                before = matrix_ref[down, across]
                after = before - product[s * NB:(s + 1) * NB, t * NB:(t + 1) * NB]
                value = jnp.where((row >= col) & (col >= 1), after, before)
                if t == 0:
                    block = tall[s * NB:(s + 1) * NB, :]
                    if i == 0 and s == 0:
                        block = jnp.where(row == 0, lower_ref[...], block)
                    value = jnp.where(col == 0, block, value)
                new[down, across] = value
        pltpu.make_async_copy(new.at[here[i]], out_ref.at[here[i]], out_sems.at[i]).start()
    for i in range(tiles):
        pltpu.make_async_copy(new.at[here[i]], out_ref.at[here[i]], out_sems.at[i]).wait()


def update(lower, inverses, matrix, panels, mirrors, plan):
    height, width = matrix.shape
    tiles = height // TILE
    vmem = pl.BlockSpec(memory_space=pltpu.VMEM)
    return pl.pallas_call(
        functools.partial(update_kernel, plan),
        out_shape=jax.ShapeDtypeStruct(matrix.shape, jnp.float32),
        in_specs=[vmem] * (4 + len(mirrors) + len(panels)),
        out_specs=pl.BlockSpec(memory_space=pl.ANY),
        scratch_shapes=[
            pltpu.VMEM((height, width), jnp.float32),
            pltpu.VMEM((height, NB), jnp.float32),
            pltpu.VMEM((width, NB), jnp.float32),
            pltpu.VMEM((width, 3 * NB), jnp.bfloat16),
            pltpu.SemaphoreType.DMA((tiles,)),
        ],
        compiler_params=pltpu.CompilerParams(vmem_limit_bytes=28 * 1024 * 1024),
        cost_estimate=pl.CostEstimate(flops=2 * height * width * NB * 3,
                                      bytes_accessed=8 * height * width, transcendentals=0),
        name="update",
    )(lower, *inverses, matrix, *mirrors, *panels)

def body(matrix):
    rows_here = lax.axis_size("row")
    cols_here = lax.axis_size("col")
    row_index = lax.axis_index("row")
    col_index = lax.axis_index("col")
    sources = rows_here // cols_here
    every_row = range(rows_here)
    odd_rows = range(1, rows_here, 2)
    last = cols_here - 1

    def send(value, pairs):
        return lax.ppermute(value, AXES, [(a * cols_here + b, c * cols_here + d) for (a, b), (c, d) in pairs])

    lower, inverse, column, first = factor(matrix, matrix.shape[1] // sources)
    lower = jnp.where((row_index == 0) & (col_index == 0), lower, 0.0)

    mirror = send(first, [((r, 0), (r | 1, r % cols_here)) for r in every_row])

    panels = [None] * last
    straight = []
    merged = column
    step = 1
    while step < cols_here:
        base = [(r, c) for r in every_row for c in range(step)]
        near = send(merged, [((r, c), (r, c + step)) for r, c in base])
        far = send(merged, [((r, c), (r, c + 2 * step)) for r, c in base])
        both = near + far
        straight += [both]
        relayed = send(both, [((r, c + step * (1 + r % 2)), (r, c + 3 * step)) for r, c in base])
        straight += []
        for c in range(step):
            panels[c + step - 1], panels[c + 2 * step - 1], panels[c + 3 * step - 1] = near, far, relayed
        merged = merged + near + far + relayed if step > 1 else (
            jnp.where(col_index == 0, column, 0.0) + near + far + relayed)
        step *= 4

    inverse = send(inverse, [((0, 0), (0, last))])
    holders = [(0, last)]
    hops = [(1 << b, 0) for b in reversed(range(1, rows_here.bit_length() - 1))]
    hops += [(0, 1 << b) for b in range(cols_here.bit_length() - 1)]
    along = [inverse]
    for dr, dc in hops:
        if len(along) == len(hops):
            inverse = lax.optimization_barrier((inverse, *straight))[0]
        moved = [(r + dr, c - dc) for r, c in holders]
        inverse = inverse + send(inverse, list(zip(holders, moved)))
        holders = holders + moved
        along.append(inverse)

    mirror, lower = lax.optimization_barrier((mirror, lower, along[1]))[:2]
    holders = [((c + q * cols_here) | 1, c) for c in range(cols_here) for q in range(sources)]
    for bit in (1 << b for b in range(1, cols_here.bit_length() - 1)):
        moved = [(r ^ bit, c) for r, c in holders]
        mirror = mirror + send(mirror, list(zip(holders, moved)))
        holders = holders + moved
    mirror = jnp.concatenate([mirror] + [
        send(mirror, [(((r + q * cols_here) % rows_here, c), (r, c)) for r, c in holders])
        for q in range(1, sources)], axis=0)
    mirror = lax.optimization_barrier((mirror, inverse))[0]

    down = [((r, c), (r - 1, c)) for r in odd_rows for c in range(cols_here)]
    mirrors = [send(mirror, down), mirror]
    inverses = [inverse, send(inverse, [(b, a) for a, b in down])]
    return update(lower, inverses, matrix, panels, mirrors, (rows_here, cols_here, sources))


def solution(mesh):
    return jax.shard_map(
        body,
        mesh=mesh,
        in_specs=(P("row", "col"),),
        out_specs=P("row", "col"),
        check_vma=False,
    )
```

```python
import functools

import jax
import jax.numpy as jnp
from jax import lax
from jax.experimental import pallas as pl
from jax.experimental.pallas import tpu as pltpu
from jax.sharding import PartitionSpec as P

NB = 128
TILE = 256
AXES = ("row", "col")
TRANS_B = (((1,), (1,)), ((), ()))


def factor_kernel(matrix_ref, lower_ref, inverse_ref, column_ref, half_ref, corner_ref, sems):
    works = (lax.axis_index("row") == 0) & (lax.axis_index("col") == 0)
    first = pl.ds(0, NB)
    copies = [
        pltpu.make_async_copy(matrix_ref.at[first, first], corner_ref, sems.at[0]),
        pltpu.make_async_copy(matrix_ref.at[pl.ds(0, half_ref.shape[0]), first], half_ref, sems.at[1]),
        pltpu.make_async_copy(matrix_ref.at[:, first], column_ref, sems.at[2]),
    ]
    for copy in copies:
        copy.start()
    copies[0].wait()

    @pl.when(works)
    def _():
        eliminate(corner_ref, lower_ref, inverse_ref)

    for copy in copies[1:]:
        copy.wait()


def eliminate(corner_ref, lower_ref, inverse_ref):
    blocks = NB // 8
    rows = lax.broadcasted_iota(jnp.int32, (NB, NB), 0)
    cols = lax.broadcasted_iota(jnp.int32, (NB, NB), 1)
    sub = lax.broadcasted_iota(jnp.int32, (8, NB), 0)
    corner = corner_ref[...]
    left = jnp.where(rows >= cols, corner, corner.T)
    right = jnp.where(rows == cols, 1.0, 0.0).astype(jnp.float32)
    lefts = [left[8 * b:8 * b + 8, :] for b in range(blocks)]
    rights = [right[8 * b:8 * b + 8, :] for b in range(blocks)]

    def whole(row):
        return jnp.broadcast_to(row, (8, NB))

    for b in range(blocks):
        def spread(i, b=b):
            return [jnp.broadcast_to(lefts[i][:, 8 * b + j:8 * b + j + 1], (8, NB)) for j in range(8)]

        here = spread(b)
        inverse_pivots, pivot_rows = [], []
        for k in range(8):
            inverse_pivots.append(1.0 / whole(here[k][k:k + 1, :]))
            pivot_rows.append([whole(column[k:k + 1, :]) for column in here])
            mult = jnp.where(sub > k, here[k] * inverse_pivots[k], 0.0)
            for j in range(k + 1, 8):
                here[j] = here[j] - mult * pivot_rows[k][j]
            lefts[b] = lefts[b] - mult * lefts[b][k:k + 1, :]
            rights[b] = rights[b] - mult * rights[b][k:k + 1, :]
        left_rows = [whole(lefts[b][k:k + 1, :]) for k in range(8)]
        right_rows = [whole(rights[b][k:k + 1, :]) for k in range(8)]
        for i in range(b + 1, blocks):
            there = spread(i)
            for k in range(8):
                mult = there[k] * inverse_pivots[k]
                for j in range(k + 1, 8):
                    there[j] = there[j] - mult * pivot_rows[k][j]
                lefts[i] = lefts[i] - mult * left_rows[k]
                rights[i] = rights[i] - mult * right_rows[k]
    upper = jnp.concatenate(lefts, axis=0)
    unit_inverse = jnp.concatenate(rights, axis=0)
    diagonal = jnp.sum(jnp.where(rows == cols, upper, 0.0), axis=1, keepdims=True)
    scale = 1.0 / jnp.sqrt(jnp.broadcast_to(diagonal, (NB, NB)))
    lower_ref[...] = jnp.where(rows >= cols, (upper * scale).T, 0.0)
    inverse_ref[...] = jnp.where(rows >= cols, unit_inverse * scale, 0.0)


def factor(matrix, half):
    square = jax.ShapeDtypeStruct((NB, NB), jnp.float32)
    tall = [jax.ShapeDtypeStruct((rows, NB), jnp.float32) for rows in (matrix.shape[0], half)]
    return pl.pallas_call(
        factor_kernel,
        out_shape=[square, square, *tall],
        in_specs=[pl.BlockSpec(memory_space=pltpu.HBM)],
        out_specs=[pl.BlockSpec(memory_space=pltpu.VMEM)] * 2 + [pl.BlockSpec(memory_space=pltpu.VMEM)] * 2,
        scratch_shapes=[pltpu.VMEM((NB, NB), jnp.float32), pltpu.SemaphoreType.DMA((3,))],
        compiler_params=pltpu.CompilerParams(vmem_limit_bytes=62 * 1024 * 1024),
        cost_estimate=pl.CostEstimate(flops=4_000_000, bytes_accessed=200_000, transcendentals=0),
        name="factor",
    )(matrix)


def split(value):
    high = value.astype(jnp.bfloat16)
    low = (value - high.astype(jnp.float32)).astype(jnp.bfloat16)
    return high, low


def dot_t(a, b):
    return lax.dot_general(a, b, TRANS_B, preferred_element_type=jnp.float32)


def left_parts(value):
    high, low = split(value)
    return jnp.concatenate([high, low, high], axis=1)


def right_parts(value):
    high, low = split(value)
    return jnp.concatenate([high, high, low], axis=1)


def update_kernel(plan, lower_ref, inverse_ref, inverse_from_ref, matrix_ref, mirror_even_ref, mirror_odd_ref, *refs):
    rows_here, cols_here, sources = plan
    panel_refs = refs[:cols_here - 1]
    out_ref, new, panel, mirror, rhs, out_sems = refs[cols_here - 1:]
    row_index = lax.axis_index("row")
    col_index = lax.axis_index("col")
    height, width = matrix_ref.shape
    col_blocks = width // NB
    each = mirror.shape[0] // sources
    tiles = height // TILE
    here = [pl.ds(i * TILE, TILE) for i in range(tiles)]
    odd = lax.rem(row_index, 2) == 1

    for q in range(sources):
        away = lax.rem(q - row_index // cols_here + sources, sources)
        for mirror_ref, here_if in [(mirror_odd_ref, odd), (mirror_even_ref, jnp.logical_not(odd))]:
            @pl.when(here_if)
            def _(q=q, away=away, mirror_ref=mirror_ref):
                mirror[pl.ds(q * each, each), :] = mirror_ref[pl.ds(pl.multiple_of(away * each, each), each), :]

    @pl.when(col_index == 0)
    def _():
        panel[...] = matrix_ref[:, pl.ds(0, NB)]

    for c in range(1, cols_here):
        @pl.when(col_index == c)
        def _(c=c):
            panel[...] = panel_refs[c - 1][...]

    inverse_parts = right_parts(inverse_ref[...] + inverse_from_ref[...])
    for t in range(col_blocks):
        block = (t % sources) * each + (t // sources) * NB
        rhs[pl.ds(t * NB, NB), :] = right_parts(dot_t(left_parts(mirror[pl.ds(block, NB), :]), inverse_parts))

    for i in range(tiles):
        tall = dot_t(left_parts(panel[here[i], :]), inverse_parts)
        product = dot_t(left_parts(tall), rhs[...])
        for s in range(TILE // NB):
            row = (i * (TILE // NB) + s) * rows_here + row_index
            down = pl.ds(i * TILE + s * NB, NB)
            for t in range(col_blocks):
                across = pl.ds(t * NB, NB)
                col = t * cols_here + col_index
                before = matrix_ref[down, across]
                after = before - product[s * NB:(s + 1) * NB, t * NB:(t + 1) * NB]
                value = jnp.where((row >= col) & (col >= 1), after, before)
                if t == 0:
                    block = tall[s * NB:(s + 1) * NB, :]
                    if i == 0 and s == 0:
                        block = jnp.where(row == 0, lower_ref[...], block)
                    value = jnp.where(col == 0, block, value)
                new[down, across] = value
        pltpu.make_async_copy(new.at[here[i]], out_ref.at[here[i]], out_sems.at[i]).start()
    for i in range(tiles):
        pltpu.make_async_copy(new.at[here[i]], out_ref.at[here[i]], out_sems.at[i]).wait()


def update(lower, inverses, matrix, panels, mirrors, plan):
    height, width = matrix.shape
    tiles = height // TILE
    vmem = pl.BlockSpec(memory_space=pltpu.VMEM)
    return pl.pallas_call(
        functools.partial(update_kernel, plan),
        out_shape=jax.ShapeDtypeStruct(matrix.shape, jnp.float32),
        in_specs=[vmem] * (4 + len(mirrors) + len(panels)),
        out_specs=pl.BlockSpec(memory_space=pl.ANY),
        scratch_shapes=[
            pltpu.VMEM((height, width), jnp.float32),
            pltpu.VMEM((height, NB), jnp.float32),
            pltpu.VMEM((width, NB), jnp.float32),
            pltpu.VMEM((width, 3 * NB), jnp.bfloat16),
            pltpu.SemaphoreType.DMA((tiles,)),
        ],
        compiler_params=pltpu.CompilerParams(vmem_limit_bytes=28 * 1024 * 1024),
        cost_estimate=pl.CostEstimate(flops=2 * height * width * NB * 3,
                                      bytes_accessed=8 * height * width, transcendentals=0),
        name="update",
    )(lower, *inverses, matrix, *mirrors, *panels)

def body(matrix):
    rows_here = lax.axis_size("row")
    cols_here = lax.axis_size("col")
    row_index = lax.axis_index("row")
    col_index = lax.axis_index("col")
    sources = rows_here // cols_here
    every_row = range(rows_here)
    odd_rows = range(1, rows_here, 2)
    last = cols_here - 1

    def send(value, pairs):
        return lax.ppermute(value, AXES, [(a * cols_here + b, c * cols_here + d) for (a, b), (c, d) in pairs])

    lower, inverse, column, first = factor(matrix, matrix.shape[1] // sources)
    lower = jnp.where((row_index == 0) & (col_index == 0), lower, 0.0)

    mirror = send(first, [((r, 0), (r | 1, r % cols_here)) for r in every_row])

    panels = [None] * last
    straight = []
    merged = column
    step = 1
    while step < cols_here:
        base = [(r, c) for r in every_row for c in range(step)]
        near = send(merged, [((r, c), (r, c + step)) for r, c in base])
        far = send(merged, [((r, c), (r, c + 2 * step)) for r, c in base])
        both = near + far
        straight += [both]
        relayed = send(both, [((r, c + step * (1 + r % 2)), (r, c + 3 * step)) for r, c in base])
        straight += []
        for c in range(step):
            panels[c + step - 1], panels[c + 2 * step - 1], panels[c + 3 * step - 1] = near, far, relayed
        merged = merged + near + far + relayed if step > 1 else (
            jnp.where(col_index == 0, column, 0.0) + near + far + relayed)
        step *= 4

    inverse = send(inverse, [((0, 0), (0, last))])
    holders = [(0, last)]
    hops = [(1 << b, 0) for b in reversed(range(1, rows_here.bit_length() - 1))]
    hops += [(0, 1 << b) for b in range(cols_here.bit_length() - 1)]
    along = [inverse]
    for dr, dc in hops:
        if len(along) == len(hops):
            inverse = lax.optimization_barrier((inverse, *straight))[0]
        moved = [(r + dr, c - dc) for r, c in holders]
        inverse = inverse + send(inverse, list(zip(holders, moved)))
        holders = holders + moved
        along.append(inverse)

    mirror, lower = lax.optimization_barrier((mirror, lower, along[1]))[:2]
    holders = [((c + q * cols_here) | 1, c) for c in range(cols_here) for q in range(sources)]
    for bit in (1 << b for b in range(1, cols_here.bit_length() - 1)):
        moved = [(r ^ bit, c) for r, c in holders]
        mirror = mirror + send(mirror, list(zip(holders, moved)))
        holders = holders + moved
    mirror = jnp.concatenate([mirror] + [
        send(mirror, [(((r + q * cols_here) % rows_here, c), (r, c)) for r, c in holders])
        for q in range(1, sources)], axis=0)
    mirror = lax.optimization_barrier((mirror, inverse))[0]

    down = [((r, c), (r - 1, c)) for r in odd_rows for c in range(cols_here)]
    mirrors = [send(mirror, down), mirror]
    inverses = [inverse, send(inverse, [(b, a) for a, b in down])]
    return update(lower, inverses, matrix, panels, mirrors, (rows_here, cols_here, sources))


def solution(mesh):
    return jax.shard_map(
        body,
        mesh=mesh,
        in_specs=(P("row", "col"),),
        out_specs=P("row", "col"),
        check_vma=False,
    )
```
